32 devices in a mesh: iface: 8 (over z, core), sub: 4 (over y, x).
Axes of the slice: x: 2, y: 2, z: 4, core: 2. Of those that a mesh axis runs over, the one named last changes fastest.
Arguments:
- traces: bfloat16 [8, 32, 256, 256], P('iface', 'sub'), may hold values from -6 to 6
- elem_count: int32 [8, 32], P('iface', 'sub'), may hold values from 16 to 64, as said below
- near_idx: int32 [8, 32, 7], P('iface', 'sub'), may hold values from 0 to 31, as said below
- near_count: int32 [8, 32], P('iface', 'sub'), may hold values from 2 to 7, as said below
- near_blocks: bfloat16 [8, 32, 7, 256, 256], P('iface', 'sub'), may hold values from -0.125 to 0.125
- source_map: bfloat16 [8, 32, 128, 256], P('iface', 'sub'), may hold values from -0.125 to 0.125
- m2l_idx: int32 [8, 4, 3], P('iface', 'sub'), may hold values from 0 to 3, as said below
- m2l_count: int32 [8, 4], P('iface', 'sub'), may hold values from 2 to 3, as said below
- translate: bfloat16 [8, 4, 3, 128, 128], P('iface', 'sub'), may hold values from -0.3125 to 0.3125
- evaluate: bfloat16 [8, 32, 256, 128], P('iface', 'sub'), may hold values from -0.5 to 0.5
- send_idx: int32 [8, 4, 2, 4, 16], P('iface', 'sub'), may hold values from 0 to 511
- recv_idx: int32 [8, 4, 2, 4, 16], P('iface', 'sub'), may hold values from 0 to 511
- recv_count: int32 [8, 4, 2, 4], P('iface', 'sub'), may hold values from 0 to 16, as said below
- couple_weight: float32 [8, 4, 2, 4, 16], P('iface', 'sub'), may hold values from 0.25 to 2
Outputs:
- calderon: bfloat16 [8, 32, 256, 256], P('iface', 'sub')
The draws below stay inside these ranges and needn't reach their ends.
Inputs may be any that keep to these rules, and one draw needn't show every extreme that they name: `near_idx`: each slot names a leaf of the same cluster at most 3 leaves from its own; slot 0 is the leaf 3 before and slot 1 the leaf 3 after, clipped to the cluster. `near_count`: some leaf of every cluster has all slots live. `elem_count`: some leaf of every cluster is full. `m2l_idx`: the slots of a box name every other box of its cluster once each. `m2l_count`: some box of every cluster has all slots live. `recv_count`: for every receiving box and side, one sending box fills all 16 slots.
All inputs are finite; a program needn't handle non-finite values.
Results may differ from the reference program's by a relative error of at most 0.0044.
Values may be sent and summed in bfloat16 or wider, within the bound.
No kernel may reach another device: no remote copies, remote signals or barrier semaphores. Data moves between devices by JAX's collectives and lax.ppermute only.
A program may use at most 64 MiB of HBM per device.

```python
import math
import jax
import jax.numpy as jnp
from jax import lax

LEAF = 64
Q = 128
NRHS = 256
LEAVES_DEV = 8
REACH = 3
NEAR = 7
SL = 16
GROUPS = 8
BOXES = 4
GL = 32
M2L = 3
ELEMS = 512


def forced_full(key, counts, highest):
    groups = counts.shape[0]
    flat = counts.reshape(groups, -1)
    place = jax.random.randint(key, (groups,), 0, flat.shape[1])
    flat = flat.at[jnp.arange(groups), place].set(highest)
    return flat.reshape(counts.shape).astype(jnp.int32)


def draw_elem_count(key, part):
    base_key = jax.random.fold_in(key, 101)
    counts = jax.random.randint(base_key, (GROUPS, GL), LEAF // 4, LEAF + 1)
    return forced_full(jax.random.fold_in(key, 102), counts, LEAF)


def draw_near_idx(key, part):
    base_key = jax.random.fold_in(key, 201)
    offsets = jax.random.randint(base_key, (GROUPS, GL, NEAR), -REACH, REACH + 1)
    offsets = offsets.at[:, :, 0].set(-REACH).at[:, :, 1].set(REACH)
    leaf_ids = jnp.arange(GL, dtype=jnp.int32)[None, :, None]
    return jnp.clip(leaf_ids + offsets, 0, GL - 1).astype(jnp.int32)


def draw_near_count(key, part):
    base_key = jax.random.fold_in(key, 301)
    counts = jax.random.randint(base_key, (GROUPS, GL), 2, NEAR + 1)
    return forced_full(jax.random.fold_in(key, 302), counts, NEAR)


def draw_m2l_idx(key, part):
    base_key = jax.random.fold_in(key, 401)
    scores = jax.random.randint(base_key, (GROUPS, BOXES, M2L), 0, 1 << 20) * M2L + jnp.arange(M2L, dtype=jnp.int32)
    ranking = jnp.argsort(scores, axis=-1, stable=True).astype(jnp.int32)
    box_ids = jnp.arange(BOXES, dtype=jnp.int32)[None, :, None]
    return (ranking + (ranking >= box_ids).astype(jnp.int32)).astype(jnp.int32)


def draw_m2l_count(key, part):
    base_key = jax.random.fold_in(key, 501)
    counts = jax.random.randint(base_key, (GROUPS, BOXES), (M2L + 1) // 2, M2L + 1)
    return forced_full(jax.random.fold_in(key, 502), counts, M2L)


def draw_send_idx(key, part):
    base_key = jax.random.fold_in(key, 601)
    return jax.random.randint(base_key, (GROUPS, BOXES, 2, BOXES, SL), 0, ELEMS).astype(jnp.int32)


def draw_recv_idx(key, part):
    base_key = jax.random.fold_in(key, 701)
    return jax.random.randint(base_key, (GROUPS, BOXES, 2, BOXES, SL), 0, ELEMS).astype(jnp.int32)


def draw_recv_count(key, part):
    base_key = jax.random.fold_in(key, 801)
    counts = jax.random.randint(base_key, (GROUPS, BOXES, 2, BOXES), 0, SL + 1)
    place = jax.random.randint(jax.random.fold_in(key, 802), (GROUPS, BOXES, 2), 0, BOXES)
    sender = jnp.arange(BOXES, dtype=jnp.int32)[None, None, None, :]
    return jnp.where(sender == place[..., None], SL, counts).astype(jnp.int32)


def shard_levels(rng, shape, cuts, smallest, largest):
    factor_of = 1.0
    for axis_at, shards_of in cuts:
        heights = jax.random.uniform(jax.random.fold_in(jax.random.fold_in(rng, 6), axis_at), (shards_of,), jnp.float32, smallest / len(cuts), largest / len(cuts))
        factor_of = factor_of * jnp.repeat(jnp.exp(heights), shape[axis_at] // shards_of).reshape((-1,) + (1,) * (len(shape) - 1 - axis_at))
    return factor_of


def normal_values(stream_key, extent, scale, reach, cuts=(), held_as=jnp.bfloat16):
    result = jax.random.normal(stream_key, extent, jnp.float32) * scale
    if len(cuts) > 0:
        result = shard_levels(stream_key, extent, cuts, -0.22, 0.18) * result
    return jnp.clip(result, min=-reach, max=reach).astype(held_as)


def setup_inputs(seed: int = 0) -> dict:
    seeds = jax.random.split(jax.random.key(seed), 15)
    return {
        "traces": normal_values(seeds[0], (GROUPS, GL, 4 * LEAF, NRHS), 1.0, 6.0, ((0, 8), (1, 4))),
        "elem_count": draw_elem_count(jax.random.fold_in(seeds[14], 71), 0),
        "near_idx": draw_near_idx(jax.random.fold_in(seeds[14], 71), 0),
        "near_count": draw_near_count(jax.random.fold_in(seeds[14], 71), 0),
        "near_blocks": normal_values(seeds[4], (GROUPS, GL, NEAR, 4 * LEAF, 4 * LEAF), (4 * LEAF * NEAR) ** -0.5, 0.125, ((0, 8), (1, 4))),
        "source_map": normal_values(seeds[5], (GROUPS, GL, Q, 4 * LEAF), (4 * LEAF * LEAVES_DEV) ** -0.5, 0.125, ((0, 8), (1, 4))),
        "m2l_idx": draw_m2l_idx(jax.random.fold_in(seeds[14], 71), 0),
        "m2l_count": draw_m2l_count(jax.random.fold_in(seeds[14], 71), 0),
        "translate": normal_values(seeds[8], (GROUPS, BOXES, M2L, Q, Q), (Q * M2L) ** -0.5, 0.3125, ((0, 8), (1, 4))),
        "evaluate": normal_values(seeds[9], (GROUPS, GL, 4 * LEAF, Q), Q ** -0.5, 0.5, ((0, 8), (1, 4))),
        "send_idx": draw_send_idx(jax.random.fold_in(seeds[14], 71), 0),
        "recv_idx": draw_recv_idx(jax.random.fold_in(seeds[14], 71), 0),
        "recv_count": draw_recv_count(jax.random.fold_in(seeds[14], 71), 0),
        "couple_weight": jnp.clip(jnp.exp(math.log(2.0) - 2.0794415 * jax.random.uniform(seeds[13], (GROUPS, BOXES, 2, BOXES, SL), jnp.float32) ** shard_levels(seeds[13], (GROUPS, BOXES, 2, BOXES, SL), ((0, 8), (1, 4)), -0.2, 0.2)), 0.25, 2.0),
    }


def reference(traces, elem_count, near_idx, near_count, near_blocks, source_map, m2l_idx, m2l_count, translate, evaluate, send_idx, recv_idx, recv_count, couple_weight):
    positions = jnp.arange(LEAF, dtype=jnp.int32)
    live_leaf = positions[None, None, :] < elem_count[:, :, None]
    live_rows = jnp.tile(live_leaf, (1, 1, 4))
    masked = jnp.where(live_rows[..., None], traces, jnp.zeros((), traces.dtype))

    def one_group(pieces):
        group_x, group_near, group_count, group_blocks, group_source, group_m2l, group_mcount, group_trans, group_eval = pieces
        picked = group_x[group_near]
        slot_live = jnp.arange(NEAR, dtype=jnp.int32)[None, :] < group_count[:, None]
        picked = jnp.where(slot_live[:, :, None, None], picked, jnp.zeros((), picked.dtype))
        near_part = jnp.einsum('lsij,lsjn->lin', group_blocks.astype(jnp.float32), picked.astype(jnp.float32))
        leaf_moment = jnp.einsum('lqj,ljn->lqn', group_source.astype(jnp.float32), group_x.astype(jnp.float32))
        box_moment = leaf_moment.reshape(BOXES, LEAVES_DEV, Q, NRHS).sum(axis=1).astype(jnp.bfloat16)
        chosen = box_moment[group_m2l]
        m2l_live = jnp.arange(M2L, dtype=jnp.int32)[None, :] < group_mcount[:, None]
        chosen = jnp.where(m2l_live[:, :, None, None], chosen, jnp.zeros((), chosen.dtype))
        box_local = jnp.einsum('bmpq,bmqn->bpn', group_trans.astype(jnp.float32), chosen.astype(jnp.float32)).astype(jnp.bfloat16)
        per_leaf = jnp.repeat(box_local, LEAVES_DEV, axis=0)
        far_part = jnp.einsum('liq,lqn->lin', group_eval.astype(jnp.float32), per_leaf.astype(jnp.float32))
        return near_part + far_part

    local_parts = lax.map(one_group, (masked, near_idx, near_count, near_blocks, source_map, m2l_idx, m2l_count, translate, evaluate))

    elements = masked.reshape(GROUPS, BOXES, LEAVES_DEV, 4, LEAF, NRHS).transpose(0, 1, 2, 4, 3, 5).reshape(GROUPS, BOXES, ELEMS, 4, NRHS)
    group_ids = jnp.arange(GROUPS, dtype=jnp.int32)[:, None, None, None, None]
    box_ids = jnp.arange(BOXES, dtype=jnp.int32)[None, :, None, None, None]
    outgoing = elements[group_ids, box_ids, send_idx]
    zero_slab = jnp.zeros_like(outgoing[:1])
    from_left = jnp.concatenate([zero_slab, outgoing[:-1]], axis=0)[:, :, 1]
    from_right = jnp.concatenate([outgoing[1:], zero_slab], axis=0)[:, :, 0]
    arrived = jnp.stack([from_left, from_right], axis=2).transpose(0, 3, 2, 1, 4, 5, 6)
    slot_valid = jnp.arange(SL, dtype=jnp.int32)[None, None, None, None, :] < recv_count[..., None]
    weights = jnp.where(slot_valid, couple_weight, jnp.zeros((), jnp.float32))
    sign_row = jnp.array([1.0, 1.0, -1.0, -1.0], dtype=jnp.float32)
    scaled = arrived.astype(jnp.float32) * weights[..., None, None] * sign_row[:, None]
    iface_el = jnp.zeros((GROUPS, BOXES, ELEMS, 4, NRHS), jnp.float32).at[group_ids, box_ids, recv_idx].add(scaled)
    iface_part = iface_el.reshape(GROUPS, BOXES, LEAVES_DEV, LEAF, 4, NRHS).transpose(0, 1, 2, 4, 3, 5).reshape(GROUPS, GL, 4 * LEAF, NRHS)
    total = local_parts + iface_part
    return jnp.where(live_rows[..., None], total, jnp.zeros((), jnp.float32)).astype(jnp.bfloat16)
```

```python
import functools

import jax
import jax.numpy as jnp
from jax import lax
from jax.experimental import pallas as pl
from jax.experimental.pallas import tpu as pltpu
from jax.sharding import PartitionSpec as P

REACH = 3
MIB = 1 << 20
F32 = jnp.float32
BF16 = jnp.bfloat16


def dot(a, b):
    return jnp.dot(a, b, preferred_element_type=F32)


def live_rows(count, leaf_size, rows, fields):
    row = lax.broadcasted_iota(jnp.int32, (rows, fields), 0)
    return lax.rem(row, leaf_size) < count


def pack_kernel(sides, owners, slots, count_ref, send_ref, x_ref, source_ref, out_ref, xm_ref):
    leaves, rows, fields = x_ref.shape
    leaf_size = rows // 4
    moment = jnp.zeros((source_ref.shape[1], fields), F32)
    picks = []
    send = send_ref[...]
    total = sides * owners * slots
    for l in range(leaves):
        live = live_rows(count_ref[0, l], leaf_size, rows, fields)
        x = jnp.where(live, x_ref[l].astype(F32), 0.0).astype(BF16)
        xm_ref[l] = x
        moment += dot(source_ref[l], x)
        element = lax.broadcasted_iota(jnp.int32, (total, leaf_size), 1) + l * leaf_size
        picks.append(jnp.where(element == send, 1.0, 0.0).astype(BF16))
    pick = jnp.concatenate(picks, axis=1)
    for c in range(4):
        comp = xm_ref[:, c * leaf_size : (c + 1) * leaf_size, :]
        got = dot(pick, comp.reshape(leaves * leaf_size, fields)).astype(BF16)
        for s in range(sides):
            for o in range(owners):
                at = (s * owners + o) * slots
                base = (s * 4 + c) * slots
                out_ref[o, base : base + slots, :] = got[at : at + slots]
    moment = moment.astype(BF16)
    for o in range(owners):
        out_ref[o, sides * 4 * slots :, :] = moment


def apply_kernel(
    boxes,
    slots,
    count_ref,
    table_ref,
    m2l_ref,
    m2l_count_ref,
    recv_ref,
    weight_ref,
    x_ref,
    near_ref,
    first_ref,
    second_ref,
    moment_ref,
    translate_ref,
    evaluate_ref,
    left_ref,
    right_ref,
    out_ref,
    src_ref,
    part_ref,
):
    leaves, rows, fields = x_ref.shape
    leaf_size = rows // 4
    near_slots = near_ref.shape[1]
    for l in range(leaves):
        live = live_rows(count_ref[0, l], leaf_size, rows, fields)
        src_ref[l] = jnp.where(live, x_ref[l].astype(F32), 0.0).astype(BF16)
    for i in range(REACH):
        src_ref[leaves + i] = first_ref[i]
        src_ref[leaves + REACH + i] = second_ref[i]
    src_ref[leaves + 2 * REACH] = jnp.zeros((rows, fields), BF16)

    local = jnp.zeros((translate_ref.shape[1], fields), F32)
    q = moment_ref.shape[1] - 8 * slots
    for t in range(translate_ref.shape[0]):
        moment = moment_ref[m2l_ref[0, t], 8 * slots :, :]
        moment = jnp.where(t < m2l_count_ref[0, 0], moment.astype(F32), 0.0).astype(BF16)
        local += dot(translate_ref[t], moment)
    local = local.astype(BF16)

    slot_total = recv_ref.shape[1]
    weight = weight_ref[...]
    high = weight.astype(BF16).astype(F32)
    low = weight - high
    element = lax.broadcasted_iota(jnp.int32, (leaves * leaf_size, slot_total), 0)
    hit = element == recv_ref[...]
    spread = jnp.concatenate(
        [jnp.where(hit, high, 0.0).astype(BF16), jnp.where(hit, low, 0.0).astype(BF16)], axis=1
    )
    for c in range(4):
        comp = [
            ref[:, c * slots : (c + 1) * slots, :].reshape(boxes * slots, fields)
            for ref in (left_ref, right_ref)
        ]
        arrived = jnp.concatenate(comp + comp, axis=0)
        part = dot(spread, arrived)
        part = part if c < 2 else -part
        part_ref[:, c * leaf_size : (c + 1) * leaf_size, :] = part.reshape(
            leaves, leaf_size, fields
        )

    def one_leaf(l, carry):
        total = dot(evaluate_ref[l], local) + part_ref[l]
        for s in range(near_slots):
            total += dot(near_ref[l, s], src_ref[table_ref[l, s]])
        live = live_rows(count_ref[0, l], leaf_size, rows, fields)
        out_ref[l] = jnp.where(live, total, 0.0).astype(BF16)
        return carry

    lax.fori_loop(0, leaves, one_leaf, 0)


def smem():
    return pl.BlockSpec(memory_space=pltpu.SMEM)


def vmem():
    return pl.BlockSpec(memory_space=pltpu.VMEM)


def shards(
    traces,
    elem_count,
    near_idx,
    near_count,
    near_blocks,
    source_map,
    m2l_idx,
    m2l_count,
    translate,
    evaluate,
    send_idx,
    recv_idx,
    recv_count,
    couple_weight,
):
    x = traces[0]
    leaves, rows, fields = x.shape
    leaf_size = rows // 4
    q = source_map.shape[2]
    sides, owners, slots = send_idx.shape[2:]
    near_slots = near_idx.shape[2]
    groups = lax.axis_size("iface")
    boxes = lax.axis_size("sub")
    me = lax.axis_index("sub")
    odd = lax.rem(me, 2)

    def edge(start):
        piece = lax.dynamic_slice_in_dim(x, start, REACH, 0)
        count = lax.dynamic_slice_in_dim(elem_count[0], start, REACH, 0)
        row = lax.broadcasted_iota(jnp.int32, (REACH, rows, fields), 1)
        return jnp.where(row % leaf_size < count[:, None, None], piece, jnp.zeros((), BF16))

    last = leaves - REACH
    pairs = [(b, b ^ 1) for b in range(boxes) if b ^ 1 < boxes]
    first = lax.ppermute(edge(jnp.where(odd == 0, last, 0)), "sub", pairs)
    up = [(b, b + 1) for b in range(1, boxes - 1, 2)]
    second = lax.ppermute(
        edge(jnp.where(odd == 0, 0, last)), "sub", up + [(j, i) for i, j in up]
    )

    chunk_rows = sides * 4 * slots
    chunks = pl.pallas_call(
        functools.partial(pack_kernel, sides, owners, slots),
        out_shape=jax.ShapeDtypeStruct((owners, chunk_rows + q, fields), BF16),
        in_specs=[smem(), vmem(), vmem(), vmem()],
        out_specs=vmem(),
        scratch_shapes=[pltpu.VMEM((leaves, rows, fields), BF16)],
        compiler_params=pltpu.CompilerParams(vmem_limit_bytes=24 * MIB),
        cost_estimate=pl.CostEstimate(flops=3 * 10**8, bytes_accessed=2 * MIB, transcendentals=0),
        name="pack",
    )(elem_count, send_idx.reshape(-1, 1), x, source_map[0])
    owned = lax.all_to_all(chunks, "sub", split_axis=0, concat_axis=0, tiled=True)
    half = chunk_rows // 2
    left = lax.ppermute(owned[:, half:chunk_rows], "iface", [(g, g + 1) for g in range(groups - 1)])
    right = lax.ppermute(owned[:, :half], "iface", [(g + 1, g) for g in range(groups - 1)])

    near = near_idx[0] - me * leaves
    low = jnp.where(odd == 0, leaves + REACH, leaves)
    high = jnp.where(odd == 0, leaves, leaves + REACH)
    table = jnp.where(near < 0, near + REACH + low, jnp.where(near < leaves, near, near - leaves + high))
    slot_at = lax.broadcasted_iota(jnp.int32, (leaves, near_slots), 1)
    table = jnp.where(slot_at < near_count[0][:, None], table, leaves + 2 * REACH)
    valid = lax.broadcasted_iota(jnp.int32, (sides, boxes, slots), 2) < recv_count[0, 0][:, :, None]
    weight = jnp.where(valid, couple_weight[0, 0], jnp.zeros((), F32)).reshape(1, -1)

    out = pl.pallas_call(
        functools.partial(apply_kernel, boxes, slots),
        out_shape=jax.ShapeDtypeStruct((leaves, rows, fields), BF16),
        in_specs=[smem(), smem(), smem(), smem()] + [vmem()] * 11,
        out_specs=vmem(),
        scratch_shapes=[
            pltpu.VMEM((leaves + 2 * REACH + 1, rows, fields), BF16),
            pltpu.VMEM((leaves, rows, fields), F32),
        ],
        compiler_params=pltpu.CompilerParams(vmem_limit_bytes=48 * MIB),
        cost_estimate=pl.CostEstimate(flops=24 * 10**8, bytes_accessed=12 * MIB, transcendentals=0),
        name="apply",
    )(
        elem_count,
        table,
        m2l_idx[0],
        m2l_count,
        recv_idx.reshape(1, -1),
        weight,
        x,
        near_blocks[0],
        first,
        second,
        owned,
        translate[0, 0],
        evaluate[0],
        left,
        right,
    )
    return out[None]


def solution(mesh):
    def split(rank):
        return P("iface", "sub", *(None,) * (rank - 2))

    return jax.shard_map(
        shards,
        mesh=mesh,
        in_specs=tuple(split(rank) for rank in (4, 2, 3, 2, 5, 4, 3, 2, 5, 4, 5, 5, 4, 5)),
        out_specs=split(4),
        check_vma=False,
    )
```

```python
import functools

import jax
import jax.numpy as jnp
from jax import lax
from jax.experimental import pallas as pl
from jax.experimental.pallas import tpu as pltpu
from jax.sharding import PartitionSpec as P

REACH = 3
MIB = 1 << 20
F32 = jnp.float32
BF16 = jnp.bfloat16
INT = jnp.int32
COST = pl.CostEstimate(flops=1, bytes_accessed=1, transcendentals=0)


def dot(a, b):
    return jnp.dot(a, b, preferred_element_type=F32)


def live_rows(count, leaf_size, fields):
    return lax.broadcasted_iota(INT, (leaf_size, fields), 0) < count


def masked_leaf(x, count):
    rows, fields = x.shape
    live = jnp.where(live_rows(count, rows // 4, fields), 1.0, 0.0).astype(BF16)
    return (x.reshape(4, rows // 4, fields) * live[None]).reshape(rows, fields)


def column(values):
    width = values.shape[-1]
    wide = values.astype(F32).reshape(-1, 1, width)
    shape = (wide.shape[0], width, width)
    same = lax.broadcasted_iota(INT, shape, 1) == lax.broadcasted_iota(INT, shape, 2)
    return jnp.sum(jnp.where(same, wide, 0.0), axis=2, keepdims=True).reshape(-1, 1)


def row(col):
    n = col.shape[0]
    same = lax.broadcasted_iota(INT, (n, n), 0) == lax.broadcasted_iota(INT, (n, n), 1)
    return jnp.sum(jnp.where(same, col, 0.0), axis=0, keepdims=True)


def load(pairs, sems):
    copies = [pltpu.make_async_copy(a, b, sems.at[i]) for i, (a, b) in enumerate(pairs)]
    for copy in copies:
        copy.start()
    return copies


def box_of(place, boxes):
    return lax.rem(place, boxes)


def pack_kernel(square, *refs):
    place_hbm, count_hbm, send_hbm, x_hbm, source_hbm = refs[:5]
    outs, (place_ref, count_ref, send_ref, x_ref, source_ref, sems) = refs[5:-6], refs[-6:]
    pair_ref, other_ref = outs[:2]
    leaves, rows, fields = x_ref.shape
    leaf_size = rows // 4
    sides, boxes, slots = send_ref.shape
    q = source_ref.shape[1]
    copies = load(
        [
            (place_hbm, place_ref),
            (count_hbm, count_ref),
            (x_hbm.at[0], x_ref),
            (send_hbm.at[0, 0], send_ref),
            (source_hbm.at[0], source_ref),
        ],
        sems,
    )
    for copy in copies[:4]:
        copy.wait()
    me = box_of(place_ref[0], boxes)
    for l in range(leaves):
        x_ref[l] = masked_leaf(x_ref[l], count_ref[0, l])

    last = leaves - REACH
    odd = lax.rem(me, 2)
    for i in range(REACH):
        pair_ref[i] = x_ref[(1 - odd) * last + i]
        other_ref[i] = x_ref[odd * last + i]

    flip = me if square else 0
    index = [send_ref[s, pl.ds(r ^ flip, 1), :] for s in range(sides) for r in range(boxes)]
    send = column(jnp.concatenate(index, axis=0)).astype(INT)
    part = 4 * slots
    moment_at = []
    if square:
        across_ref, own_ref, self_ref = outs[2:]
        targets = [(self_ref, 0), (across_ref, q + sides * part), (own_ref, q), (across_ref, q)]
        moment_at = [across_ref.at[0:q], own_ref.at[0:q]]
    else:
        targets = [(outs[2].at[o], 0) for o in range(boxes)]
        moment_at = [outs[2].at[o, sides * part :] for o in range(boxes)]
    total = sides * boxes * slots
    element = lax.broadcasted_iota(INT, (total, leaves * leaf_size), 1)
    pick = jnp.where(element == send, 1.0, 0.0).astype(BF16)
    for c in range(4):
        comp = x_ref[:, c * leaf_size : (c + 1) * leaf_size, :]
        got = dot(pick, comp.reshape(leaves * leaf_size, fields)).astype(BF16)
        for s in range(sides):
            for r, (ref, base) in enumerate(targets):
                at = (s * boxes + r) * slots
                to = base + s * part + c * slots
                ref[to : to + slots, :] = got[at : at + slots]
    copies[4].wait()
    blocks = jnp.concatenate([source_ref[l] for l in range(leaves)], axis=1)
    moment = dot(blocks, x_ref[...].reshape(leaves * rows, fields)).astype(BF16)
    for ref in moment_at:
        ref[...] = moment


def local_kernel(
    square,
    place_hbm,
    count_hbm,
    idx_hbm,
    live_hbm,
    recv_hbm,
    recv_count_hbm,
    weight_hbm,
    x_hbm,
    near_hbm,
    acc_ref,
    rows_ref,
    near_ref,
    place_ref,
    count_ref,
    idx_ref,
    live_ref,
    recv_ref,
    recv_count_ref,
    weight_ref,
    src_ref,
    sems,
    near_sems,
):
    leaves, rows, fields = acc_ref.shape
    near_slots = idx_ref.shape[0]
    sides, boxes, slots = recv_ref.shape
    copies = load(
        [
            (place_hbm, place_ref),
            (count_hbm, count_ref),
            (x_hbm.at[0], src_ref.at[0:leaves]),
            (idx_hbm, idx_ref),
            (live_hbm, live_ref),
            (recv_hbm.at[0, 0], recv_ref),
            (recv_count_hbm.at[0, 0], recv_count_ref),
            (weight_hbm.at[0, 0], weight_ref),
        ],
        sems,
    )
    near_copies = load([(near_hbm.at[0, l], near_ref.at[l]) for l in range(leaves)], near_sems)
    src_ref[leaves] = jnp.zeros((rows, fields), BF16)
    for copy in copies:
        copy.wait()
    for l in range(leaves):
        src_ref[l] = masked_leaf(src_ref[l], count_ref[0, l])

    me = box_of(place_ref[0], boxes)
    flip = me if square else 0
    weights, targets = [], []
    for s in range(sides):
        for r in range(boxes):
            b = r ^ flip
            live = lax.broadcasted_iota(INT, (1, slots), 1) < recv_count_ref[s, b]
            weights.append(jnp.where(live, weight_ref[s, pl.ds(b, 1), :], 0.0))
            targets.append(recv_ref[s, pl.ds(b, 1), :])
    weight = row(column(jnp.concatenate(weights, axis=0)))
    upper = weight.astype(BF16).astype(F32)
    rows_ref[0:1, :] = row(column(jnp.concatenate(targets, axis=0)))
    rows_ref[1:2, :] = upper
    rows_ref[2:3, :] = weight - upper

    start = me * leaves
    for l in range(leaves):
        if l % 4 == 0:
            for copy in near_copies[l : l + 4]:
                copy.wait()
        blocks, sources = [], []
        for s in range(near_slots):
            at = idx_ref[s, 0, l] - start
            used = (s < live_ref[0, l]) & (at >= 0) & (at < leaves)
            blocks.append(near_ref[l, s])
            sources.append(src_ref[jnp.where(used, at, leaves)])
        acc_ref[l] = dot(jnp.concatenate(blocks, axis=1), jnp.concatenate(sources, axis=0))


def final_kernel(square, *refs):
    (
        place_hbm,
        count_hbm,
        idx_hbm,
        live_hbm,
        m2l_hbm,
        m2l_count_hbm,
        near_hbm,
        translate_hbm,
        evaluate_hbm,
        acc_ref,
        rows_ref,
        first_ref,
        direct_ref,
        turned_ref,
        left_ref,
        right_ref,
    ) = refs[:16]
    (
        out_hbm,
        place_ref,
        count_ref,
        idx_ref,
        live_ref,
        m2l_ref,
        m2l_count_ref,
        translate_ref,
        evaluate_ref,
        moment_ref,
        near_ref,
        halo_ref,
        out_ref,
        part_ref,
        sems,
        near_sems,
        out_sems,
    ) = refs[-17:]
    moments = refs[16:-17]
    leaves, rows, fields = acc_ref.shape
    leaf_size = rows // 4
    near_slots = idx_ref.shape[0]
    boxes, part, _ = left_ref.shape
    slots = part // 4
    q = translate_ref.shape[1]
    copies = load(
        [
            (place_hbm, place_ref),
            (idx_hbm, idx_ref),
            (live_hbm, live_ref),
            (count_hbm, count_ref),
            (m2l_hbm, m2l_ref),
            (m2l_count_hbm, m2l_count_ref),
            (translate_hbm.at[0, 0], translate_ref),
            (evaluate_hbm.at[0], evaluate_ref),
        ],
        sems,
    )
    zero_block = leaves * near_slots
    near_ref[zero_block] = jnp.zeros((rows, rows), BF16)
    halo_ref[2 * REACH] = jnp.zeros((rows, fields), BF16)
    for i in range(REACH):
        halo_ref[i] = first_ref[i]
    if square:
        own_ref, across_ref, beyond_ref = moments
        for r, (ref, at) in enumerate(
            [(own_ref, 0), (across_ref, 0), (beyond_ref, 0), (beyond_ref, q + 2 * part)]
        ):
            moment_ref[r] = ref[at : at + q]
    else:
        for r in range(boxes):
            moment_ref[r] = moments[0][r, 2 * part :]
    for copy in copies[:3]:
        copy.wait()

    place = place_ref[0]
    me = box_of(place, boxes)
    odd = lax.rem(me, 2)
    start = me * leaves
    low = REACH + (1 - odd) * REACH
    high = odd * REACH - leaves
    outer = [l for l in range(leaves) if l < REACH or l >= leaves - REACH]

    def slot(l, s):
        at = idx_ref[s, 0, l] - start
        used = (s < live_ref[0, l]) & ((at < 0) | (at >= leaves))
        return used, at + jnp.where(at < 0, low, high)

    def block_copy(l, s):
        n = l * near_slots + s
        return pltpu.make_async_copy(near_hbm.at[0, l, s], near_ref.at[n], near_sems.at[n])

    for l in outer:
        for s in range(near_slots):

            @pl.when(slot(l, s)[0])
            def _(l=l, s=s):
                block_copy(l, s).start()

    slot_total = rows_ref.shape[1]
    element = lax.broadcasted_iota(INT, (leaves * leaf_size, slot_total), 0)
    hit = element == rows_ref[0:1, :].astype(INT)
    spread = jnp.concatenate(
        [jnp.where(hit, rows_ref[i : i + 1, :], 0.0).astype(BF16) for i in (1, 2)], axis=1
    )
    for c in range(4):
        comp = [
            ref[:, c * slots : (c + 1) * slots, :].reshape(boxes * slots, fields)
            for ref in (left_ref, right_ref)
        ]
        sums = dot(spread, jnp.concatenate(comp + comp, axis=0))
        sums = sums if c < 2 else -sums
        part_ref[:, c * leaf_size : (c + 1) * leaf_size, :] = sums.reshape(
            leaves, leaf_size, fields
        )

    for copy in copies[3:]:
        copy.wait()
    flip = me if square else 0
    local = jnp.zeros((q, fields), F32)
    for t in range(translate_ref.shape[0]):
        moment = moment_ref[m2l_ref[0, 0, t] ^ flip]
        moment = jnp.where(t < m2l_count_ref[0, 0], moment.astype(F32), 0.0).astype(BF16)
        local += dot(translate_ref[t], moment)
    local = local.astype(BF16)

    relayed = place >= boxes
    for flag, ref in ((relayed, turned_ref), (jnp.logical_not(relayed), direct_ref)):

        @pl.when(flag)
        def _(ref=ref):
            for i in range(REACH):
                halo_ref[REACH + i] = ref[i]

    for l in outer:
        for s in range(near_slots):

            @pl.when(slot(l, s)[0])
            def _(l=l, s=s):
                block_copy(l, s).wait()

    stores = []
    for l in range(leaves):
        blocks, sources = [evaluate_ref[l]], [local]
        if l in outer:
            for s in range(near_slots):
                used, at = slot(l, s)
                blocks.append(near_ref[jnp.where(used, l * near_slots + s, zero_block)])
                sources.append(halo_ref[jnp.where(used, at, 2 * REACH)])
        total = dot(jnp.concatenate(blocks, axis=1), jnp.concatenate(sources, axis=0))
        total = (total + acc_ref[l] + part_ref[l]).reshape(4, leaf_size, fields)
        live = live_rows(count_ref[0, l], leaf_size, fields)
        out_ref[l] = jnp.where(live[None], total, 0.0).astype(BF16).reshape(rows, fields)
        stores.append(pltpu.make_async_copy(out_ref.at[l], out_hbm.at[l], out_sems.at[l]))
        stores[-1].start()
    for store in stores:
        store.wait()


def vmem():
    return pl.BlockSpec(memory_space=pltpu.VMEM)


def hbm():
    return pl.BlockSpec(memory_space=pltpu.MemorySpace.HBM)


def pin(x):
    return pltpu.with_memory_space_constraint(x, pltpu.MemorySpace.HBM)


def shards(
    traces,
    elem_count,
    near_idx,
    near_count,
    near_blocks,
    source_map,
    m2l_idx,
    m2l_count,
    translate,
    evaluate,
    send_idx,
    recv_idx,
    recv_count,
    couple_weight,
):
    leaves, rows, fields = traces.shape[1:]
    q = source_map.shape[2]
    sides, _, slots = send_idx.shape[2:]
    near_slots = near_idx.shape[2]
    groups = lax.axis_size("iface")
    boxes = lax.axis_size("sub")
    part = 4 * slots
    slot_total = sides * boxes * slots
    square = boxes == 4
    place = lax.axis_index("sub")
    if square:
        place = place + boxes * lax.rem(lax.axis_index("iface"), 2)
    place = place.reshape(1)

    params = pltpu.CompilerParams(vmem_limit_bytes=24 * MIB)
    piece = jax.ShapeDtypeStruct((REACH, rows, fields), BF16)
    if square:
        shapes = [(q + 2 * sides * part, fields), (q + sides * part, fields), (sides * part, fields)]
    else:
        shapes = [(boxes, sides * part + q, fields)]
    to_pair, to_other, *packed = pl.pallas_call(
        functools.partial(pack_kernel, square),
        out_shape=[piece, piece] + [jax.ShapeDtypeStruct(shape, BF16) for shape in shapes],
        in_specs=[hbm()] * 5,
        out_specs=[vmem()] * (2 + len(shapes)),
        scratch_shapes=[
            pltpu.SMEM((1,), INT),
            pltpu.SMEM((1, leaves), INT),
            pltpu.VMEM(send_idx.shape[2:], INT),
            pltpu.VMEM((leaves, rows, fields), BF16),
            pltpu.VMEM((leaves, q, rows), BF16),
            pltpu.SemaphoreType.DMA((5,)),
        ],
        compiler_params=params,
        cost_estimate=COST,
        name="pack",
    )(place, pin(elem_count), pin(send_idx), pin(traces), pin(source_map))

    def flips(bit):
        return [(b, b ^ bit) for b in range(boxes) if b ^ bit < boxes]

    def clusters(chosen, sub_pairs):
        return [(g * boxes + i, g * boxes + j) for g in chosen for i, j in sub_pairs]

    axes = ("iface", "sub")
    every = range(groups)
    across = [(b, b + 1) for b in range(1, boxes - 1, 2)]
    across = across + [(j, i) for i, j in across]
    up = [(g, g + 1) for g in range(groups - 1)]
    down = [(g + 1, g) for g in range(groups - 1)]
    near_at = pin(near_idx.transpose(2, 0, 1))

    def local_sums(place):
        return pl.pallas_call(
            functools.partial(local_kernel, square),
            out_shape=(
                jax.ShapeDtypeStruct((leaves, rows, fields), F32),
                jax.ShapeDtypeStruct((8, slot_total), F32),
            ),
            in_specs=[hbm()] * 9,
            out_specs=(vmem(),) * 2,
            scratch_shapes=[
                pltpu.VMEM(near_blocks.shape[1:], BF16),
                pltpu.SMEM((1,), INT),
                pltpu.SMEM((1, leaves), INT),
                pltpu.SMEM((near_slots, 1, leaves), INT),
                pltpu.SMEM((1, leaves), INT),
                pltpu.VMEM((sides, boxes, slots), INT),
                pltpu.SMEM((sides, boxes), INT),
                pltpu.VMEM((sides, boxes, slots), F32),
                pltpu.VMEM((leaves + 1, rows, fields), BF16),
                pltpu.SemaphoreType.DMA((8,)),
                pltpu.SemaphoreType.DMA((leaves,)),
            ],
            compiler_params=params,
            cost_estimate=COST,
            name="local",
        )(
            place,
            pin(elem_count),
            near_at,
            pin(near_count),
            pin(recv_idx),
            pin(recv_count),
            pin(couple_weight),
            pin(traces),
            pin(near_blocks),
        )

    if square:
        to_across, own, mine = packed
        from_across = lax.ppermute(to_across, "sub", flips(1))
        first = lax.ppermute(to_pair, "sub", flips(1))
        hop = lax.ppermute(to_other, axes, clusters(every[1::2], [(1, 3), (2, 0)]))
        direct = lax.ppermute(to_other, axes, clusters(every[::2], across))
        both = jnp.concatenate([own, from_across[: q + sides * part]], axis=0)
        beyond = lax.ppermute(both, "sub", flips(2))
        turned = lax.ppermute(
            hop, axes, clusters(every[1::2], [(3, 2), (0, 1)])
        )
        acc, slot_rows = local_sums(place)
        beyond = lax.optimization_barrier((beyond, slot_rows))[0]
        owned = []
        for s in range(sides):
            at = [(mine, 0), (from_across, q + sides * part), (beyond, q), (beyond, 2 * q + sides * part)]
            owned.append(
                jnp.concatenate([x[i + s * part : i + (s + 1) * part] for x, i in at], axis=0)
            )
        to_next, to_prev = (x.reshape(boxes, part, fields) for x in (owned[1], owned[0]))
        moments = (own, from_across, beyond)
    else:
        first = lax.ppermute(to_pair, "sub", flips(1))
        direct = lax.ppermute(to_other, "sub", across)
        turned = direct
        acc, slot_rows = local_sums(place)
        owned = lax.all_to_all(packed[0], "sub", split_axis=0, concat_axis=0, tiled=True)
        to_prev, to_next = owned[:, :part], owned[:, part : 2 * part]
        moments = (owned,)
    left = lax.ppermute(to_next, "iface", up)
    right = lax.ppermute(to_prev, "iface", down)

    out = pl.pallas_call(
        functools.partial(final_kernel, square),
        out_shape=jax.ShapeDtypeStruct((leaves, rows, fields), BF16),
        in_specs=[hbm()] * 9 + [vmem()] * (7 + len(moments)),
        out_specs=hbm(),
        scratch_shapes=[
            pltpu.SMEM((1,), INT),
            pltpu.SMEM((1, leaves), INT),
            pltpu.SMEM((near_slots, 1, leaves), INT),
            pltpu.SMEM((1, leaves), INT),
            pltpu.SMEM((1, 1, translate.shape[2]), INT),
            pltpu.SMEM((1, 1), INT),
            pltpu.VMEM(translate.shape[2:], BF16),
            pltpu.VMEM((leaves, rows, q), BF16),
            pltpu.VMEM((boxes, q, fields), BF16),
            pltpu.VMEM((leaves * near_slots + 1, rows, rows), BF16),
            pltpu.VMEM((2 * REACH + 1, rows, fields), BF16),
            pltpu.VMEM((leaves, rows, fields), BF16),
            pltpu.VMEM((leaves, rows, fields), F32),
            pltpu.SemaphoreType.DMA((8,)),
            pltpu.SemaphoreType.DMA((leaves * near_slots,)),
            pltpu.SemaphoreType.DMA((leaves,)),
        ],
        compiler_params=params,
        cost_estimate=COST,
        name="final",
    )(
        place,
        pin(elem_count),
        near_at,
        pin(near_count),
        pin(m2l_idx),
        m2l_count,
        pin(near_blocks),
        pin(translate),
        pin(evaluate),
        acc,
        slot_rows,
        first,
        direct,
        turned,
        left,
        right,
        *moments,
    )
    return out[None]


def solution(mesh):
    def split(rank):
        return P("iface", "sub", *(None,) * (rank - 2))

    return jax.shard_map(
        shards,
        mesh=mesh,
        in_specs=tuple(split(rank) for rank in (4, 2, 3, 2, 5, 4, 3, 2, 5, 4, 5, 5, 4, 5)),
        out_specs=split(4),
        check_vma=False,
    )
```

```python
import functools

import jax
import jax.numpy as jnp
from jax import lax
from jax.experimental import pallas as pl
from jax.experimental.pallas import tpu as pltpu
from jax.sharding import PartitionSpec as P

REACH = 3
MIB = 1 << 20
F32 = jnp.float32
BF16 = jnp.bfloat16
INT = jnp.int32
GROUP = 4
COST = pl.CostEstimate(flops=1, bytes_accessed=1, transcendentals=0)


def dot(a, b):
    return jnp.dot(a, b, preferred_element_type=F32)


def live_rows(count, leaf_size, fields):
    return lax.broadcasted_iota(INT, (leaf_size, fields), 0) < count


def masked_leaf(x, count):
    rows, fields = x.shape
    live = jnp.where(live_rows(count, rows // 4, fields), 1.0, 0.0).astype(BF16)
    return (x.reshape(4, rows // 4, fields) * live[None]).reshape(rows, fields)


def column(values):
    width = values.shape[-1]
    wide = values.astype(F32).reshape(-1, 1, width)
    shape = (wide.shape[0], width, width)
    same = lax.broadcasted_iota(INT, shape, 1) == lax.broadcasted_iota(INT, shape, 2)
    return jnp.sum(jnp.where(same, wide, 0.0), axis=2, keepdims=True).reshape(-1, 1)


def row(col):
    n = col.shape[0]
    same = lax.broadcasted_iota(INT, (n, n), 0) == lax.broadcasted_iota(INT, (n, n), 1)
    return jnp.sum(jnp.where(same, col, 0.0), axis=0, keepdims=True)


def load(pairs, sems):
    copies = [pltpu.make_async_copy(a, b, sems.at[i]) for i, (a, b) in enumerate(pairs)]
    for copy in copies:
        copy.start()
    return copies


def box_of(place, boxes):
    return lax.rem(place, boxes)


def met_side(place, boxes):
    return jnp.where(place < boxes, 1, 0)


def edge_kernel(boxes, place_hbm, count_hbm, x_hbm, pair_ref, other_ref, place_ref, count_ref, x_ref, sems):
    last = x_hbm.shape[1] - REACH
    copies = load(
        [
            (place_hbm, place_ref),
            (count_hbm, count_ref),
            (x_hbm.at[0, 0:REACH], x_ref.at[0:REACH]),
            (x_hbm.at[0, last:], x_ref.at[REACH:]),
        ],
        sems,
    )
    for copy in copies:
        copy.wait()
    odd = lax.rem(box_of(place_ref[0], boxes), 2)
    for i in range(REACH):
        for ref, upper in ((pair_ref, 1 - odd), (other_ref, odd)):
            ref[i] = masked_leaf(x_ref[upper * REACH + i], count_ref[0, upper * last + i])


def pack_kernel(
    after_hbm,
    place_hbm,
    count_hbm,
    send_hbm,
    x_hbm,
    source_hbm,
    chunk_ref,
    place_ref,
    count_ref,
    send_ref,
    x_ref,
    source_ref,
    sems,
):
    leaves, rows, fields = x_ref.shape
    leaf_size = rows // 4
    sides, boxes, slots = send_ref.shape
    copies = load(
        [
            (place_hbm, place_ref),
            (count_hbm, count_ref),
            (send_hbm.at[0, 0], send_ref),
            (x_hbm.at[0], x_ref),
            (source_hbm.at[0], source_ref),
        ],
        sems,
    )
    for copy in copies[:3]:
        copy.wait()
    met = met_side(place_ref[0], boxes)
    send = jnp.concatenate([send_ref[met], send_ref[1 - met]], axis=0)
    send = column(send).astype(INT)
    part = 4 * slots
    total = sides * boxes * slots
    element = lax.broadcasted_iota(INT, (total, leaves * leaf_size), 1)
    pick = jnp.where(element == send, 1.0, 0.0).astype(BF16)
    copies[3].wait()
    for l in range(leaves):
        x_ref[l] = masked_leaf(x_ref[l], count_ref[0, l])
    for c in range(4):
        comp = x_ref[:, c * leaf_size : (c + 1) * leaf_size, :]
        got = dot(pick, comp.reshape(leaves * leaf_size, fields)).astype(BF16)
        for s in range(sides):
            for o in range(boxes):
                at = (s * boxes + o) * slots
                to = s * part + c * slots
                chunk_ref[o, to : to + slots, :] = got[at : at + slots]
    copies[4].wait()
    blocks = jnp.concatenate([source_ref[l] for l in range(leaves)], axis=1)
    moment = dot(blocks, x_ref[...].reshape(leaves * rows, fields)).astype(BF16)
    for o in range(boxes):
        chunk_ref[o, sides * part :, :] = moment


def near_kernel(
    place_hbm,
    count_hbm,
    idx_hbm,
    live_hbm,
    recv_hbm,
    recv_count_hbm,
    weight_hbm,
    x_hbm,
    near_hbm,
    first_hbm,
    acc_ref,
    rows_ref,
    place_ref,
    count_ref,
    idx_ref,
    live_ref,
    recv_ref,
    recv_count_ref,
    weight_ref,
    near_ref,
    src_ref,
    sems,
    near_sems,
):
    leaves, rows, fields = acc_ref.shape
    leaf_size = rows // 4
    near_slots = idx_ref.shape[0]
    sides, boxes, slots = recv_ref.shape
    copies = load(
        [
            (place_hbm, place_ref),
            (count_hbm, count_ref),
            (recv_hbm.at[0, 0], recv_ref),
            (recv_count_hbm.at[0, 0], recv_count_ref),
            (weight_hbm.at[0, 0], weight_ref),
            (idx_hbm, idx_ref),
            (live_hbm, live_ref),
            (x_hbm.at[0], src_ref.at[0:leaves]),
            (first_hbm, src_ref.at[leaves : leaves + REACH]),
        ],
        sems,
    )
    near_copies = load([(near_hbm.at[0, l], near_ref.at[l]) for l in range(leaves)], near_sems)
    zero_leaf = leaves + REACH
    src_ref[zero_leaf] = jnp.zeros((rows, fields), BF16)
    for copy in copies[:7]:
        copy.wait()

    met = met_side(place_ref[0], boxes)
    weights = []
    for s in (met, 1 - met):
        for b in range(boxes):
            live = lax.broadcasted_iota(INT, (1, slots), 1) < recv_count_ref[s, b]
            weights.append(jnp.where(live, weight_ref[s, b : b + 1, :], 0.0))
    weight = row(column(jnp.concatenate(weights, axis=0)))
    target = jnp.concatenate([recv_ref[met], recv_ref[1 - met]], axis=0)
    target = row(column(target))
    upper = weight.astype(BF16).astype(F32)
    rows_ref[0:1, :] = target
    rows_ref[1:2, :] = upper
    rows_ref[2:3, :] = weight - upper

    copies[7].wait()
    copies[8].wait()
    for l in range(leaves):
        src_ref[l] = masked_leaf(src_ref[l], count_ref[0, l])
    me = box_of(place_ref[0], boxes)
    odd = lax.rem(me, 2) == 1
    start = me * leaves
    for l in range(leaves):
        if l % GROUP == 0:
            for copy in near_copies[l : l + GROUP]:
                copy.wait()
        blocks, sources = [], []
        for s in range(near_slots):
            at = idx_ref[s, 0, l] - start
            pair = jnp.where(odd, at < 0, at >= leaves)
            own = (at >= 0) & (at < leaves)
            at = at + jnp.where(pair & odd, leaves + REACH, 0)
            used = (s < live_ref[0, l]) & (own | pair)
            blocks.append(near_ref[l, s])
            sources.append(src_ref[jnp.where(used, at, zero_leaf)])
        acc_ref[l] = dot(jnp.concatenate(blocks, axis=1), jnp.concatenate(sources, axis=0))


def final_kernel(
    square,
    place_hbm,
    count_hbm,
    idx_hbm,
    live_hbm,
    m2l_hbm,
    m2l_count_hbm,
    near_hbm,
    translate_hbm,
    evaluate_hbm,
    acc_ref,
    rows_ref,
    direct_ref,
    turned_ref,
    met_ref,
    other_ref,
    owned_ref,
    out_hbm,
    place_ref,
    count_ref,
    idx_ref,
    live_ref,
    m2l_ref,
    m2l_count_ref,
    near_ref,
    translate_ref,
    evaluate_ref,
    halo_ref,
    out_ref,
    part_ref,
    sems,
    out_sems,
):
    leaves, rows, fields = out_ref.shape
    leaf_size = rows // 4
    near_slots = idx_ref.shape[0]
    boxes, part, _ = met_ref.shape
    slots = part // 4
    q = translate_ref.shape[1]
    copies = load(
        [
            (place_hbm, place_ref),
            (m2l_hbm, m2l_ref),
            (m2l_count_hbm, m2l_count_ref),
            (count_hbm, count_ref),
            (idx_hbm, idx_ref),
            (live_hbm, live_ref),
            (translate_hbm.at[0, 0], translate_ref),
            (evaluate_hbm.at[0], evaluate_ref),
        ],
        sems,
    )
    zero_leaf = REACH
    halo_ref[zero_leaf] = jnp.zeros((rows, fields), BF16)
    copies[0].wait()
    place = place_ref[0]
    me = box_of(place, boxes)
    odd = lax.rem(me, 2)
    edge = odd * (leaves - REACH)
    near_copy = pltpu.make_async_copy(near_hbm.at[0, pl.ds(edge, REACH)], near_ref, out_sems.at[0])
    near_copy.start()

    relayed = square & (place >= boxes)
    for flag, ref in ((relayed, turned_ref), (jnp.logical_not(relayed), direct_ref)):

        @pl.when(flag)
        def _(ref=ref):
            for i in range(REACH):
                halo_ref[i] = ref[i]

    slot_total = rows_ref.shape[1]
    element = lax.broadcasted_iota(INT, (leaves * leaf_size, slot_total), 0)
    hit = element == rows_ref[0:1, :].astype(INT)
    spread = jnp.concatenate(
        [jnp.where(hit, rows_ref[i : i + 1, :], 0.0).astype(BF16) for i in (1, 2)], axis=1
    )
    for c in range(4):
        comp = [
            ref[:, c * slots : (c + 1) * slots, :].reshape(boxes * slots, fields)
            for ref in (met_ref, other_ref)
        ]
        sums = dot(spread, jnp.concatenate(comp + comp, axis=0))
        sums = sums if c < 2 else -sums
        part_ref[:, c * leaf_size : (c + 1) * leaf_size, :] = sums.reshape(
            leaves, leaf_size, fields
        )

    for copy in copies[1:]:
        copy.wait()
    local = jnp.zeros((q, fields), F32)
    for t in range(translate_ref.shape[0]):
        moment = owned_ref[m2l_ref[0, 0, t], 2 * part :, :]
        moment = jnp.where(t < m2l_count_ref[0, 0], moment.astype(F32), 0.0).astype(BF16)
        local += dot(translate_ref[t], moment)
    local = local.astype(BF16)
    for l in range(leaves):
        part_ref[l] += dot(evaluate_ref[l], local) + acc_ref[l]

    near_copy.wait()
    start = me * leaves
    for i in range(REACH):
        l = edge + i
        blocks, sources = [], []
        for s in range(near_slots):
            at = idx_ref[s, 0, l] - start
            far = jnp.where(odd == 1, at >= leaves, at < 0)
            at = at + jnp.where(odd == 1, -leaves, REACH)
            blocks.append(near_ref[i, s])
            sources.append(halo_ref[jnp.where((s < live_ref[0, l]) & far, at, zero_leaf)])
        part_ref[l] += dot(jnp.concatenate(blocks, axis=1), jnp.concatenate(sources, axis=0))

    half = leaves // 2
    stores = []
    for l in range(leaves):
        total = part_ref[l].reshape(4, leaf_size, fields)
        live = live_rows(count_ref[0, l], leaf_size, fields)
        out_ref[l] = jnp.where(live[None], total, 0.0).astype(BF16).reshape(rows, fields)
        if l % half == half - 1:
            span = slice(l + 1 - half, l + 1)
            stores.append(
                pltpu.make_async_copy(out_ref.at[span], out_hbm.at[span], out_sems.at[1 + l // half])
            )
            stores[-1].start()
    for store in stores:
        store.wait()


def vmem():
    return pl.BlockSpec(memory_space=pltpu.VMEM)


def hbm():
    return pl.BlockSpec(memory_space=pltpu.MemorySpace.HBM)


def pin(x):
    return pltpu.with_memory_space_constraint(x, pltpu.MemorySpace.HBM)


def shards(
    traces,
    elem_count,
    near_idx,
    near_count,
    near_blocks,
    source_map,
    m2l_idx,
    m2l_count,
    translate,
    evaluate,
    send_idx,
    recv_idx,
    recv_count,
    couple_weight,
):
    leaves, rows, fields = traces.shape[1:]
    q = source_map.shape[2]
    sides, _, slots = send_idx.shape[2:]
    near_slots = near_idx.shape[2]
    groups = lax.axis_size("iface")
    boxes = lax.axis_size("sub")
    part = 4 * slots
    slot_total = sides * boxes * slots
    square = boxes == 4
    parity = lax.rem(lax.axis_index("iface"), 2)
    place = (lax.axis_index("sub") + boxes * parity).reshape(1)

    params = pltpu.CompilerParams(vmem_limit_bytes=24 * MIB)
    piece = jax.ShapeDtypeStruct((REACH, rows, fields), BF16)
    chunk = jax.ShapeDtypeStruct((boxes, sides * part + q, fields), BF16)
    to_pair, to_other = pl.pallas_call(
        functools.partial(edge_kernel, boxes),
        out_shape=[piece, piece],
        in_specs=[hbm()] * 3,
        out_specs=[vmem()] * 2,
        scratch_shapes=[
            pltpu.SMEM((1,), INT),
            pltpu.SMEM((1, leaves), INT),
            pltpu.VMEM((2 * REACH, rows, fields), BF16),
            pltpu.SemaphoreType.DMA((4,)),
        ],
        compiler_params=params,
        cost_estimate=COST,
        name="edges",
    )(place, pin(elem_count), pin(traces))
    chunks = pl.pallas_call(
        pack_kernel,
        out_shape=chunk,
        in_specs=[pl.BlockSpec(memory_space=pl.ANY)] + [hbm()] * 5,
        out_specs=vmem(),
        scratch_shapes=[
            pltpu.SMEM((1,), INT),
            pltpu.SMEM((1, leaves), INT),
            pltpu.VMEM(send_idx.shape[2:], INT),
            pltpu.VMEM((leaves, rows, fields), BF16),
            pltpu.VMEM((leaves, q, rows), BF16),
            pltpu.SemaphoreType.DMA((5,)),
        ],
        compiler_params=params,
        cost_estimate=COST,
        name="pack",
    )(to_pair, place, pin(elem_count), pin(send_idx), pin(traces), pin(source_map))

    def flips(bit):
        return [(b, b ^ bit) for b in range(boxes) if b ^ bit < boxes]

    def clusters(chosen, sub_pairs):
        return [(g * boxes + i, g * boxes + j) for g in chosen for i, j in sub_pairs]

    axes = ("iface", "sub")
    every = range(groups)
    across = [(b, b + 1) for b in range(1, boxes - 1, 2)]
    across = across + [(j, i) for i, j in across]
    owned = lax.all_to_all(chunks, "sub", split_axis=0, concat_axis=0, tiled=True)
    first = lax.ppermute(to_pair, "sub", flips(1))
    if square:
        hop = lax.ppermute(to_other, axes, clusters(every[1::2], [(1, 3), (2, 0)]))
        direct = lax.ppermute(to_other, axes, clusters(every[::2], across))
        turned = lax.ppermute(lax.optimization_barrier((hop, first))[0], axes, clusters(every[1::2], [(3, 2), (0, 1)]))
    else:
        direct = lax.ppermute(to_other, "sub", across)
        turned = direct
    near_at = pin(near_idx.transpose(2, 0, 1))
    slot_total = sides * boxes * slots
    acc, slot_rows = pl.pallas_call(
        near_kernel,
        out_shape=(
            jax.ShapeDtypeStruct((leaves, rows, fields), F32),
            jax.ShapeDtypeStruct((8, slot_total), F32),
        ),
        in_specs=[hbm()] * 10,
        out_specs=(vmem(), vmem()),
        scratch_shapes=[
            pltpu.SMEM((1,), INT),
            pltpu.SMEM((1, leaves), INT),
            pltpu.SMEM((near_slots, 1, leaves), INT),
            pltpu.SMEM((1, leaves), INT),
            pltpu.VMEM((sides, boxes, slots), INT),
            pltpu.SMEM((sides, boxes), INT),
            pltpu.VMEM((sides, boxes, slots), F32),
            pltpu.VMEM(near_blocks.shape[1:], BF16),
            pltpu.VMEM((leaves + REACH + 1, rows, fields), BF16),
            pltpu.SemaphoreType.DMA((9,)),
            pltpu.SemaphoreType.DMA((leaves,)),
        ],
        compiler_params=params,
        cost_estimate=COST,
        name="near",
    )(
        place,
        pin(elem_count),
        near_at,
        pin(near_count),
        pin(recv_idx),
        pin(recv_count),
        pin(couple_weight),
        pin(traces),
        pin(near_blocks),
        pin(first),
    )

    owned = lax.optimization_barrier((owned, slot_rows))[0]
    meet = [(g, g ^ 1) for g in range(groups) if g ^ 1 < groups]
    met = lax.ppermute(owned[:, :part], "iface", meet)
    turn = [(g, g + 1) for g in range(1, groups - 1, 2)]
    other = lax.ppermute(owned[:, part : 2 * part], "iface", turn + [(j, i) for i, j in turn])

    out = pl.pallas_call(
        functools.partial(final_kernel, square),
        out_shape=jax.ShapeDtypeStruct((leaves, rows, fields), BF16),
        in_specs=[hbm()] * 9 + [vmem()] * 7,
        out_specs=hbm(),
        scratch_shapes=[
            pltpu.SMEM((1,), INT),
            pltpu.SMEM((1, leaves), INT),
            pltpu.SMEM((near_slots, 1, leaves), INT),
            pltpu.SMEM((1, leaves), INT),
            pltpu.SMEM((1, 1, translate.shape[2]), INT),
            pltpu.SMEM((1, 1), INT),
            pltpu.VMEM((REACH,) + near_blocks.shape[2:], BF16),
            pltpu.VMEM(translate.shape[2:], BF16),
            pltpu.VMEM((leaves, rows, q), BF16),
            pltpu.VMEM((REACH + 1, rows, fields), BF16),
            pltpu.VMEM((leaves, rows, fields), BF16),
            pltpu.VMEM((leaves, rows, fields), F32),
            pltpu.SemaphoreType.DMA((8,)),
            pltpu.SemaphoreType.DMA((3,)),
        ],
        compiler_params=params,
        cost_estimate=COST,
        name="final",
    )(
        place,
        pin(elem_count),
        near_at,
        pin(near_count),
        pin(m2l_idx),
        m2l_count,
        pin(near_blocks),
        pin(translate),
        pin(evaluate),
        acc,
        slot_rows,
        direct,
        turned,
        met,
        other,
        owned,
    )
    return out[None]


def solution(mesh):
    def split(rank):
        return P("iface", "sub", *(None,) * (rank - 2))

    return jax.shard_map(
        shards,
        mesh=mesh,
        in_specs=tuple(split(rank) for rank in (4, 2, 3, 2, 5, 4, 3, 2, 5, 4, 5, 5, 4, 5)),
        out_specs=split(4),
        check_vma=False,
    )
```

```python
import functools

import jax
import jax.numpy as jnp
from jax import lax
from jax.experimental import pallas as pl
from jax.experimental.pallas import tpu as pltpu
from jax.sharding import PartitionSpec as P

REACH = 3
MIB = 1 << 20
F32 = jnp.float32
BF16 = jnp.bfloat16
INT = jnp.int32
GROUP = 4
COST = pl.CostEstimate(flops=1, bytes_accessed=1, transcendentals=0)


def dot(a, b):
    return jnp.dot(a, b, preferred_element_type=F32)


def live_rows(count, leaf_size, fields):
    return lax.broadcasted_iota(INT, (leaf_size, fields), 0) < count


def masked_leaf(x, count):
    rows, fields = x.shape
    live = jnp.where(live_rows(count, rows // 4, fields), 1.0, 0.0).astype(BF16)
    return (x.reshape(4, rows // 4, fields) * live[None]).reshape(rows, fields)


def column(values):
    width = values.shape[-1]
    wide = values.astype(F32).reshape(-1, 1, width)
    shape = (wide.shape[0], width, width)
    same = lax.broadcasted_iota(INT, shape, 1) == lax.broadcasted_iota(INT, shape, 2)
    return jnp.sum(jnp.where(same, wide, 0.0), axis=2, keepdims=True).reshape(-1, 1)


def row(col):
    n = col.shape[0]
    same = lax.broadcasted_iota(INT, (n, n), 0) == lax.broadcasted_iota(INT, (n, n), 1)
    return jnp.sum(jnp.where(same, col, 0.0), axis=0, keepdims=True)


def load(pairs, sems):
    copies = [pltpu.make_async_copy(a, b, sems.at[i]) for i, (a, b) in enumerate(pairs)]
    for copy in copies:
        copy.start()
    return copies


def box_of(place, boxes):
    return lax.rem(place, boxes)


def met_side(place, boxes):
    return jnp.where(place < boxes, 1, 0)


def edge_kernel(boxes, place_hbm, count_hbm, x_hbm, pair_ref, other_ref, place_ref, count_ref, x_ref, sems):
    last = x_hbm.shape[1] - REACH
    copies = load(
        [
            (place_hbm, place_ref),
            (count_hbm, count_ref),
            (x_hbm.at[0, 0:REACH], x_ref.at[0:REACH]),
            (x_hbm.at[0, last:], x_ref.at[REACH:]),
        ],
        sems,
    )
    for copy in copies:
        copy.wait()
    odd = lax.rem(box_of(place_ref[0], boxes), 2)
    for i in range(REACH):
        for ref, upper in ((pair_ref, 1 - odd), (other_ref, odd)):
            ref[i] = masked_leaf(x_ref[upper * REACH + i], count_ref[0, upper * last + i])


def pack_kernel(
    after_hbm,
    place_hbm,
    count_hbm,
    send_hbm,
    x_hbm,
    source_hbm,
    met_ref,
    other_ref,
    moment_ref,
    place_ref,
    count_ref,
    send_ref,
    x_ref,
    source_ref,
    sems,
):
    leaves, rows, fields = x_ref.shape
    leaf_size = rows // 4
    sides, boxes, slots = send_ref.shape
    copies = load(
        [
            (place_hbm, place_ref),
            (count_hbm, count_ref),
            (send_hbm.at[0, 0], send_ref),
            (x_hbm.at[0], x_ref),
            (source_hbm.at[0], source_ref),
        ],
        sems,
    )
    for copy in copies[:3]:
        copy.wait()
    met = met_side(place_ref[0], boxes)
    send = jnp.concatenate([send_ref[met], send_ref[1 - met]], axis=0)
    send = column(send).astype(INT)
    total = sides * boxes * slots
    element = lax.broadcasted_iota(INT, (total, leaves * leaf_size), 1)
    pick = jnp.where(element == send, 1.0, 0.0).astype(BF16)
    copies[3].wait()
    for l in range(leaves):
        x_ref[l] = masked_leaf(x_ref[l], count_ref[0, l])
    for c in range(4):
        comp = x_ref[:, c * leaf_size : (c + 1) * leaf_size, :]
        got = dot(pick, comp.reshape(leaves * leaf_size, fields)).astype(BF16)
        for s, ref in enumerate((met_ref, other_ref)):
            for o in range(boxes):
                at = (s * boxes + o) * slots
                ref[o, c * slots : (c + 1) * slots, :] = got[at : at + slots]
    copies[4].wait()
    blocks = jnp.concatenate([source_ref[l] for l in range(leaves)], axis=1)
    moment = dot(blocks, x_ref[...].reshape(leaves * rows, fields)).astype(BF16)
    moment_ref[...] = moment


def near_kernel(
    place_hbm,
    count_hbm,
    idx_hbm,
    live_hbm,
    recv_hbm,
    recv_count_hbm,
    weight_hbm,
    x_hbm,
    near_hbm,
    first_hbm,
    acc_ref,
    rows_ref,
    place_ref,
    count_ref,
    idx_ref,
    live_ref,
    recv_ref,
    recv_count_ref,
    weight_ref,
    near_ref,
    src_ref,
    sems,
    near_sems,
):
    leaves, rows, fields = acc_ref.shape
    leaf_size = rows // 4
    near_slots = idx_ref.shape[0]
    sides, boxes, slots = recv_ref.shape
    copies = load(
        [
            (place_hbm, place_ref),
            (count_hbm, count_ref),
            (recv_hbm.at[0, 0], recv_ref),
            (recv_count_hbm.at[0, 0], recv_count_ref),
            (weight_hbm.at[0, 0], weight_ref),
            (idx_hbm, idx_ref),
            (live_hbm, live_ref),
            (x_hbm.at[0], src_ref.at[0:leaves]),
            (first_hbm, src_ref.at[leaves : leaves + REACH]),
        ],
        sems,
    )
    near_copies = load([(near_hbm.at[0, l], near_ref.at[l]) for l in range(leaves)], near_sems)
    zero_leaf = leaves + REACH
    src_ref[zero_leaf] = jnp.zeros((rows, fields), BF16)
    for copy in copies[:7]:
        copy.wait()

    met = met_side(place_ref[0], boxes)
    weights = []
    for s in (met, 1 - met):
        for b in range(boxes):
            live = lax.broadcasted_iota(INT, (1, slots), 1) < recv_count_ref[s, b]
            weights.append(jnp.where(live, weight_ref[s, b : b + 1, :], 0.0))
    weight = row(column(jnp.concatenate(weights, axis=0)))
    target = jnp.concatenate([recv_ref[met], recv_ref[1 - met]], axis=0)
    target = row(column(target))
    upper = weight.astype(BF16).astype(F32)
    rows_ref[0:1, :] = target
    rows_ref[1:2, :] = upper
    rows_ref[2:3, :] = weight - upper

    copies[7].wait()
    copies[8].wait()
    for l in range(leaves):
        src_ref[l] = masked_leaf(src_ref[l], count_ref[0, l])
    me = box_of(place_ref[0], boxes)
    odd = lax.rem(me, 2) == 1
    start = me * leaves
    for l in range(leaves):
        if l % GROUP == 0:
            for copy in near_copies[l : l + GROUP]:
                copy.wait()
        blocks, sources = [], []
        for s in range(near_slots):
            at = idx_ref[s, 0, l] - start
            pair = jnp.where(odd, at < 0, at >= leaves)
            own = (at >= 0) & (at < leaves)
            at = at + jnp.where(pair & odd, leaves + REACH, 0)
            used = (s < live_ref[0, l]) & (own | pair)
            blocks.append(near_ref[l, s])
            sources.append(src_ref[jnp.where(used, at, zero_leaf)])
        acc_ref[l] = dot(jnp.concatenate(blocks, axis=1), jnp.concatenate(sources, axis=0))


def final_kernel(
    place_hbm,
    count_hbm,
    idx_hbm,
    live_hbm,
    m2l_hbm,
    m2l_count_hbm,
    near_hbm,
    translate_hbm,
    evaluate_hbm,
    acc_ref,
    rows_ref,
    direct_ref,
    owned_ref,
    out_hbm,
    place_ref,
    count_ref,
    idx_ref,
    live_ref,
    m2l_ref,
    m2l_count_ref,
    near_ref,
    translate_ref,
    evaluate_ref,
    halo_ref,
    out_ref,
    part_ref,
    sems,
    out_sems,
):
    leaves, rows, fields = out_ref.shape
    leaf_size = rows // 4
    near_slots = idx_ref.shape[0]
    boxes, chunk, _ = owned_ref.shape
    q = translate_ref.shape[1]
    part = (chunk - q) // 2
    slots = part // 4
    copies = load(
        [
            (place_hbm, place_ref),
            (m2l_hbm, m2l_ref),
            (m2l_count_hbm, m2l_count_ref),
            (count_hbm, count_ref),
            (idx_hbm, idx_ref),
            (live_hbm, live_ref),
            (translate_hbm.at[0, 0], translate_ref),
            (evaluate_hbm.at[0], evaluate_ref),
        ],
        sems,
    )
    zero_leaf = REACH
    halo_ref[zero_leaf] = jnp.zeros((rows, fields), BF16)
    copies[0].wait()
    place = place_ref[0]
    me = box_of(place, boxes)
    odd = lax.rem(me, 2)
    edge = odd * (leaves - REACH)
    near_copy = pltpu.make_async_copy(near_hbm.at[0, pl.ds(edge, REACH)], near_ref, out_sems.at[0])
    near_copy.start()

    for i in range(REACH):
        halo_ref[i] = direct_ref[i]

    slot_total = rows_ref.shape[1]
    element = lax.broadcasted_iota(INT, (leaves * leaf_size, slot_total), 0)
    hit = element == rows_ref[0:1, :].astype(INT)
    spread = jnp.concatenate(
        [jnp.where(hit, rows_ref[i : i + 1, :], 0.0).astype(BF16) for i in (1, 2)], axis=1
    )
    for c in range(4):
        comp = [
            owned_ref[:, at : at + slots, :].reshape(boxes * slots, fields)
            for at in (c * slots, part + c * slots)
        ]
        sums = dot(spread, jnp.concatenate(comp + comp, axis=0))
        sums = sums if c < 2 else -sums
        part_ref[:, c * leaf_size : (c + 1) * leaf_size, :] = sums.reshape(
            leaves, leaf_size, fields
        )

    for copy in copies[1:]:
        copy.wait()
    local = jnp.zeros((q, fields), F32)
    for t in range(translate_ref.shape[0]):
        moment = owned_ref[m2l_ref[0, 0, t], 2 * part :, :]
        moment = jnp.where(t < m2l_count_ref[0, 0], moment.astype(F32), 0.0).astype(BF16)
        local += dot(translate_ref[t], moment)
    local = local.astype(BF16)
    def finish(l, total):
        total = (total + acc_ref[l] + part_ref[l]).reshape(4, leaf_size, fields)
        live = live_rows(count_ref[0, l], leaf_size, fields)
        out_ref[l] = jnp.where(live[None], total, 0.0).astype(BF16).reshape(rows, fields)

    rest = (1 - odd) * REACH
    inner = leaves - REACH
    for i in range(inner):
        finish(rest + i, dot(evaluate_ref[rest + i], local))
    stores = []
    for at, size, sem in ((rest, inner, 1), (edge, REACH, 2)):
        span = pl.ds(at, size)
        stores.append(pltpu.make_async_copy(out_ref.at[span], out_hbm.at[span], out_sems.at[sem]))
    stores[0].start()

    near_copy.wait()
    start = me * leaves
    for i in range(REACH):
        l = edge + i
        blocks, sources = [], []
        for s in range(near_slots):
            at = idx_ref[s, 0, l] - start
            far = jnp.where(odd == 1, at >= leaves, at < 0)
            at = at + jnp.where(odd == 1, -leaves, REACH)
            blocks.append(near_ref[i, s])
            sources.append(halo_ref[jnp.where((s < live_ref[0, l]) & far, at, zero_leaf)])
        blocks.append(evaluate_ref[l])
        sources.append(local)
        finish(l, dot(jnp.concatenate(blocks, axis=1), jnp.concatenate(sources, axis=0)))
    stores[1].start()
    for store in stores:
        store.wait()


def vmem():
    return pl.BlockSpec(memory_space=pltpu.VMEM)


def hbm():
    return pl.BlockSpec(memory_space=pltpu.MemorySpace.HBM)


def pin(x):
    return pltpu.with_memory_space_constraint(x, pltpu.MemorySpace.HBM)


def shards(
    traces,
    elem_count,
    near_idx,
    near_count,
    near_blocks,
    source_map,
    m2l_idx,
    m2l_count,
    translate,
    evaluate,
    send_idx,
    recv_idx,
    recv_count,
    couple_weight,
):
    leaves, rows, fields = traces.shape[1:]
    q = source_map.shape[2]
    sides, _, slots = send_idx.shape[2:]
    near_slots = near_idx.shape[2]
    groups = lax.axis_size("iface")
    boxes = lax.axis_size("sub")
    part = 4 * slots
    slot_total = sides * boxes * slots
    parity = lax.rem(lax.axis_index("iface"), 2)
    place = (lax.axis_index("sub") + boxes * parity).reshape(1)

    params = pltpu.CompilerParams(vmem_limit_bytes=24 * MIB)
    piece = jax.ShapeDtypeStruct((REACH, rows, fields), BF16)
    toward = jax.ShapeDtypeStruct((boxes, part, fields), BF16)
    to_pair, to_other = pl.pallas_call(
        functools.partial(edge_kernel, boxes),
        out_shape=[piece, piece],
        in_specs=[hbm()] * 3,
        out_specs=[vmem()] * 2,
        scratch_shapes=[
            pltpu.SMEM((1,), INT),
            pltpu.SMEM((1, leaves), INT),
            pltpu.VMEM((2 * REACH, rows, fields), BF16),
            pltpu.SemaphoreType.DMA((4,)),
        ],
        compiler_params=params,
        cost_estimate=COST,
        name="edges",
    )(place, pin(elem_count), pin(traces))
    to_met, to_turn, moment = pl.pallas_call(
        pack_kernel,
        out_shape=(toward, toward, jax.ShapeDtypeStruct((q, fields), BF16)),
        in_specs=[pl.BlockSpec(memory_space=pl.ANY)] + [hbm()] * 5,
        out_specs=(vmem(),) * 3,
        scratch_shapes=[
            pltpu.SMEM((1,), INT),
            pltpu.SMEM((1, leaves), INT),
            pltpu.VMEM(send_idx.shape[2:], INT),
            pltpu.VMEM((leaves, rows, fields), BF16),
            pltpu.VMEM((leaves, q, rows), BF16),
            pltpu.SemaphoreType.DMA((5,)),
        ],
        compiler_params=params,
        cost_estimate=COST,
        name="pack",
    )(to_pair, place, pin(elem_count), pin(send_idx), pin(traces), pin(source_map))

    def flips(bit):
        return [(b, b ^ bit) for b in range(boxes) if b ^ bit < boxes]

    across = [(b, b + 1) for b in range(1, boxes - 1, 2)]
    across = across + [(j, i) for i, j in across]
    first = lax.ppermute(to_pair, "sub", flips(1))
    meet = [(g, g ^ 1) for g in range(groups) if g ^ 1 < groups]
    met = lax.ppermute(to_met, "iface", meet)
    turn = [(g, g + 1) for g in range(1, groups - 1, 2)]
    other = lax.ppermute(to_turn, "iface", turn + [(j, i) for i, j in turn])
    to_other = lax.optimization_barrier((to_other, moment))[0]
    direct = lax.ppermute(to_other, "sub", across)
    carried = lax.optimization_barrier((moment, first))[0]
    carried = jnp.broadcast_to(carried, (boxes, q, fields))
    chunks = jnp.concatenate([met, other, carried], axis=1)
    owned = lax.all_to_all(chunks, "sub", split_axis=0, concat_axis=0, tiled=True)
    near_at = pin(near_idx.transpose(2, 0, 1))
    slot_total = sides * boxes * slots
    acc, slot_rows = pl.pallas_call(
        near_kernel,
        out_shape=(
            jax.ShapeDtypeStruct((leaves, rows, fields), F32),
            jax.ShapeDtypeStruct((8, slot_total), F32),
        ),
        in_specs=[hbm()] * 10,
        out_specs=(vmem(), vmem()),
        scratch_shapes=[
            pltpu.SMEM((1,), INT),
            pltpu.SMEM((1, leaves), INT),
            pltpu.SMEM((near_slots, 1, leaves), INT),
            pltpu.SMEM((1, leaves), INT),
            pltpu.VMEM((sides, boxes, slots), INT),
            pltpu.SMEM((sides, boxes), INT),
            pltpu.VMEM((sides, boxes, slots), F32),
            pltpu.VMEM(near_blocks.shape[1:], BF16),
            pltpu.VMEM((leaves + REACH + 1, rows, fields), BF16),
            pltpu.SemaphoreType.DMA((9,)),
            pltpu.SemaphoreType.DMA((leaves,)),
        ],
        compiler_params=params,
        cost_estimate=COST,
        name="near",
    )(
        lax.optimization_barrier((place, chunks))[0],
        pin(elem_count),
        near_at,
        pin(near_count),
        pin(recv_idx),
        pin(recv_count),
        pin(couple_weight),
        pin(traces),
        pin(near_blocks),
        pin(first),
    )

    out = pl.pallas_call(
        final_kernel,
        out_shape=jax.ShapeDtypeStruct((leaves, rows, fields), BF16),
        in_specs=[hbm()] * 9 + [vmem()] * 4,
        out_specs=hbm(),
        scratch_shapes=[
            pltpu.SMEM((1,), INT),
            pltpu.SMEM((1, leaves), INT),
            pltpu.SMEM((near_slots, 1, leaves), INT),
            pltpu.SMEM((1, leaves), INT),
            pltpu.SMEM((1, 1, translate.shape[2]), INT),
            pltpu.SMEM((1, 1), INT),
            pltpu.VMEM((REACH,) + near_blocks.shape[2:], BF16),
            pltpu.VMEM(translate.shape[2:], BF16),
            pltpu.VMEM((leaves, rows, q), BF16),
            pltpu.VMEM((REACH + 1, rows, fields), BF16),
            pltpu.VMEM((leaves, rows, fields), BF16),
            pltpu.VMEM((leaves, rows, fields), F32),
            pltpu.SemaphoreType.DMA((8,)),
            pltpu.SemaphoreType.DMA((3,)),
        ],
        compiler_params=params,
        cost_estimate=COST,
        name="final",
    )(
        place,
        pin(elem_count),
        near_at,
        pin(near_count),
        pin(m2l_idx),
        m2l_count,
        pin(near_blocks),
        pin(translate),
        pin(evaluate),
        acc,
        slot_rows,
        direct,
        owned,
    )
    return out[None]


def solution(mesh):
    def split(rank):
        return P("iface", "sub", *(None,) * (rank - 2))

    return jax.shard_map(
        shards,
        mesh=mesh,
        in_specs=tuple(split(rank) for rank in (4, 2, 3, 2, 5, 4, 3, 2, 5, 4, 5, 5, 4, 5)),
        out_specs=split(4),
        check_vma=False,
    )
```

```python
import functools

import jax
import jax.numpy as jnp
from jax import lax
from jax.experimental import pallas as pl
from jax.experimental.pallas import tpu as pltpu
from jax.sharding import PartitionSpec as P

REACH = 3
MIB = 1 << 20
F32 = jnp.float32
BF16 = jnp.bfloat16
INT = jnp.int32
GROUP = 4
COST = pl.CostEstimate(flops=1, bytes_accessed=1, transcendentals=0)


def dot(a, b):
    return jnp.dot(a, b, preferred_element_type=F32)


def live_rows(count, leaf_size, fields):
    return lax.broadcasted_iota(INT, (leaf_size, fields), 0) < count


def masked_leaf(x, count):
    rows, fields = x.shape
    live = jnp.where(live_rows(count, rows // 4, fields), 1.0, 0.0).astype(BF16)
    return (x.reshape(4, rows // 4, fields) * live[None]).reshape(rows, fields)


def column(values):
    width = values.shape[-1]
    wide = values.astype(F32).reshape(-1, 1, width)
    shape = (wide.shape[0], width, width)
    same = lax.broadcasted_iota(INT, shape, 1) == lax.broadcasted_iota(INT, shape, 2)
    return jnp.sum(jnp.where(same, wide, 0.0), axis=2, keepdims=True).reshape(-1, 1)


def row(col):
    n = col.shape[0]
    same = lax.broadcasted_iota(INT, (n, n), 0) == lax.broadcasted_iota(INT, (n, n), 1)
    return jnp.sum(jnp.where(same, col, 0.0), axis=0, keepdims=True)


def load(pairs, sems):
    copies = [pltpu.make_async_copy(a, b, sems.at[i]) for i, (a, b) in enumerate(pairs)]
    for copy in copies:
        copy.start()
    return copies


def box_of(place, boxes):
    return lax.rem(place, boxes)


def met_side(place, boxes):
    return jnp.where(place < boxes, 1, 0)


def edge_kernel(boxes, place_hbm, count_hbm, x_hbm, pair_ref, other_ref, place_ref, count_ref, x_ref, sems):
    last = x_hbm.shape[1] - REACH
    copies = load(
        [
            (place_hbm, place_ref),
            (count_hbm, count_ref),
            (x_hbm.at[0, 0:REACH], x_ref.at[0:REACH]),
            (x_hbm.at[0, last:], x_ref.at[REACH:]),
        ],
        sems,
    )
    for copy in copies:
        copy.wait()
    odd = lax.rem(box_of(place_ref[0], boxes), 2)
    for i in range(REACH):
        for ref, upper in ((pair_ref, 1 - odd), (other_ref, odd)):
            ref[i] = masked_leaf(x_ref[upper * REACH + i], count_ref[0, upper * last + i])


def pack_kernel(
    after_hbm,
    place_hbm,
    count_hbm,
    send_hbm,
    x_hbm,
    source_hbm,
    met_ref,
    other_ref,
    moment_ref,
    place_ref,
    count_ref,
    send_ref,
    x_ref,
    source_ref,
    sems,
):
    leaves, rows, fields = x_ref.shape
    leaf_size = rows // 4
    sides, boxes, slots = send_ref.shape
    copies = load(
        [
            (place_hbm, place_ref),
            (count_hbm, count_ref),
            (send_hbm.at[0, 0], send_ref),
            (x_hbm.at[0], x_ref),
            (source_hbm.at[0], source_ref),
        ],
        sems,
    )
    for copy in copies[:3]:
        copy.wait()
    met = met_side(place_ref[0], boxes)
    send = jnp.concatenate([send_ref[met], send_ref[1 - met]], axis=0)
    send = column(send).astype(INT)
    total = sides * boxes * slots
    element = lax.broadcasted_iota(INT, (total, leaves * leaf_size), 1)
    pick = jnp.where(element == send, 1.0, 0.0).astype(BF16)
    copies[3].wait()
    for l in range(leaves):
        x_ref[l] = masked_leaf(x_ref[l], count_ref[0, l])
    for c in range(4):
        comp = x_ref[:, c * leaf_size : (c + 1) * leaf_size, :]
        got = dot(pick, comp.reshape(leaves * leaf_size, fields)).astype(BF16)
        for s, ref in enumerate((met_ref, other_ref)):
            for o in range(boxes):
                at = (s * boxes + o) * slots
                ref[o, c * slots : (c + 1) * slots, :] = got[at : at + slots]
    copies[4].wait()
    blocks = jnp.concatenate([source_ref[l] for l in range(leaves)], axis=1)
    moment = dot(blocks, x_ref[...].reshape(leaves * rows, fields)).astype(BF16)
    moment_ref[...] = moment


def near_kernel(
    place_hbm,
    count_hbm,
    idx_hbm,
    live_hbm,
    recv_hbm,
    recv_count_hbm,
    weight_hbm,
    x_hbm,
    near_hbm,
    first_hbm,
    acc_ref,
    rows_ref,
    place_ref,
    count_ref,
    idx_ref,
    live_ref,
    recv_ref,
    recv_count_ref,
    weight_ref,
    near_ref,
    src_ref,
    sems,
    near_sems,
):
    leaves, rows, fields = acc_ref.shape
    leaf_size = rows // 4
    near_slots = idx_ref.shape[0]
    sides, boxes, slots = recv_ref.shape
    copies = load(
        [
            (place_hbm, place_ref),
            (count_hbm, count_ref),
            (recv_hbm.at[0, 0], recv_ref),
            (recv_count_hbm.at[0, 0], recv_count_ref),
            (weight_hbm.at[0, 0], weight_ref),
            (idx_hbm, idx_ref),
            (live_hbm, live_ref),
            (x_hbm.at[0], src_ref.at[0:leaves]),
            (first_hbm, src_ref.at[leaves : leaves + REACH]),
        ],
        sems,
    )
    near_copies = load([(near_hbm.at[0, l], near_ref.at[l]) for l in range(leaves)], near_sems)
    zero_leaf = leaves + REACH
    src_ref[zero_leaf] = jnp.zeros((rows, fields), BF16)
    for copy in copies[:7]:
        copy.wait()

    met = met_side(place_ref[0], boxes)
    weights = []
    for s in (met, 1 - met):
        for b in range(boxes):
            live = lax.broadcasted_iota(INT, (1, slots), 1) < recv_count_ref[s, b]
            weights.append(jnp.where(live, weight_ref[s, b : b + 1, :], 0.0))
    weight = row(column(jnp.concatenate(weights, axis=0)))
    target = jnp.concatenate([recv_ref[met], recv_ref[1 - met]], axis=0)
    target = row(column(target))
    upper = weight.astype(BF16).astype(F32)
    rows_ref[0:1, :] = target
    rows_ref[1:2, :] = upper
    rows_ref[2:3, :] = weight - upper

    copies[7].wait()
    copies[8].wait()
    for l in range(leaves):
        src_ref[l] = masked_leaf(src_ref[l], count_ref[0, l])
    me = box_of(place_ref[0], boxes)
    odd = lax.rem(me, 2) == 1
    start = me * leaves
    for l in range(leaves):
        if l % GROUP == 0:
            for copy in near_copies[l : l + GROUP]:
                copy.wait()
        blocks, sources = [], []
        for s in range(near_slots):
            at = idx_ref[s, 0, l] - start
            pair = jnp.where(odd, at < 0, at >= leaves)
            own = (at >= 0) & (at < leaves)
            at = at + jnp.where(pair & odd, leaves + REACH, 0)
            used = (s < live_ref[0, l]) & (own | pair)
            blocks.append(near_ref[l, s])
            sources.append(src_ref[jnp.where(used, at, zero_leaf)])
        acc_ref[l] = dot(jnp.concatenate(blocks, axis=1), jnp.concatenate(sources, axis=0))


def final_kernel(
    place_hbm,
    count_hbm,
    idx_hbm,
    live_hbm,
    m2l_hbm,
    m2l_count_hbm,
    near_hbm,
    translate_hbm,
    evaluate_hbm,
    acc_ref,
    rows_ref,
    direct_ref,
    owned_ref,
    out_hbm,
    place_ref,
    count_ref,
    idx_ref,
    live_ref,
    m2l_ref,
    m2l_count_ref,
    near_ref,
    translate_ref,
    evaluate_ref,
    halo_ref,
    out_ref,
    part_ref,
    sems,
    out_sems,
):
    leaves, rows, fields = out_ref.shape
    leaf_size = rows // 4
    near_slots = idx_ref.shape[0]
    boxes, chunk, _ = owned_ref.shape
    q = translate_ref.shape[1]
    part = (chunk - q) // 2
    slots = part // 4
    copies = load(
        [
            (place_hbm, place_ref),
            (m2l_hbm, m2l_ref),
            (m2l_count_hbm, m2l_count_ref),
            (count_hbm, count_ref),
            (idx_hbm, idx_ref),
            (live_hbm, live_ref),
            (translate_hbm.at[0, 0], translate_ref),
            (evaluate_hbm.at[0], evaluate_ref),
        ],
        sems,
    )
    zero_leaf = REACH
    halo_ref[zero_leaf] = jnp.zeros((rows, fields), BF16)
    copies[0].wait()
    place = place_ref[0]
    me = box_of(place, boxes)
    odd = lax.rem(me, 2)
    edge = odd * (leaves - REACH)
    near_copy = pltpu.make_async_copy(near_hbm.at[0, pl.ds(edge, REACH)], near_ref, out_sems.at[0])
    near_copy.start()

    for i in range(REACH):
        halo_ref[i] = direct_ref[i]

    slot_total = rows_ref.shape[1]
    element = lax.broadcasted_iota(INT, (leaves * leaf_size, slot_total), 0)
    hit = element == rows_ref[0:1, :].astype(INT)
    spread = jnp.concatenate(
        [jnp.where(hit, rows_ref[i : i + 1, :], 0.0).astype(BF16) for i in (1, 2)], axis=1
    )
    for c in range(4):
        comp = [
            owned_ref[:, at : at + slots, :].reshape(boxes * slots, fields)
            for at in (c * slots, part + c * slots)
        ]
        sums = dot(spread, jnp.concatenate(comp + comp, axis=0))
        sums = sums if c < 2 else -sums
        part_ref[:, c * leaf_size : (c + 1) * leaf_size, :] = sums.reshape(
            leaves, leaf_size, fields
        )

    for copy in copies[1:]:
        copy.wait()
    local = jnp.zeros((q, fields), F32)
    for t in range(translate_ref.shape[0]):
        moment = owned_ref[m2l_ref[0, 0, t], 2 * part :, :]
        moment = jnp.where(t < m2l_count_ref[0, 0], moment.astype(F32), 0.0).astype(BF16)
        local += dot(translate_ref[t], moment)
    local = local.astype(BF16)
    def finish(l, total):
        total = (total + acc_ref[l] + part_ref[l]).reshape(4, leaf_size, fields)
        live = live_rows(count_ref[0, l], leaf_size, fields)
        out_ref[l] = jnp.where(live[None], total, 0.0).astype(BF16).reshape(rows, fields)

    start = me * leaves
    inner = leaves - REACH

    def sums(parity):
        first_far = parity * inner
        rest = (1 - parity) * REACH
        stores = []

        def store(at, size):
            span = slice(at, at + size)
            copy = pltpu.make_async_copy(
                out_ref.at[span], out_hbm.at[span], out_sems.at[1 + len(stores)]
            )
            copy.start()
            stores.append(copy)

        for l in range(rest, rest + inner):
            finish(l, dot(evaluate_ref[l], local))
        store(rest, inner)
        near_copy.wait()
        for i in range(REACH):
            l = first_far + i
            blocks, sources = [], []
            for s in range(near_slots):
                at = idx_ref[s, 0, l] - start
                far = at >= leaves if parity else at < 0
                at = at + (-leaves if parity else REACH)
                used = (s < live_ref[0, l]) & far
                blocks.append(near_ref[i, s])
                sources.append(halo_ref[jnp.where(used, at, zero_leaf)])
            blocks.append(evaluate_ref[l])
            sources.append(local)
            finish(l, dot(jnp.concatenate(blocks, axis=1), jnp.concatenate(sources, axis=0)))
            store(l, 1)
        for copy in stores:
            copy.wait()

    for parity in (0, 1):
        pl.when(odd == parity)(functools.partial(sums, parity))


def vmem():
    return pl.BlockSpec(memory_space=pltpu.VMEM)


def hbm():
    return pl.BlockSpec(memory_space=pltpu.MemorySpace.HBM)


def pin(x):
    return pltpu.with_memory_space_constraint(x, pltpu.MemorySpace.HBM)


def shards(
    traces,
    elem_count,
    near_idx,
    near_count,
    near_blocks,
    source_map,
    m2l_idx,
    m2l_count,
    translate,
    evaluate,
    send_idx,
    recv_idx,
    recv_count,
    couple_weight,
):
    leaves, rows, fields = traces.shape[1:]
    q = source_map.shape[2]
    sides, _, slots = send_idx.shape[2:]
    near_slots = near_idx.shape[2]
    groups = lax.axis_size("iface")
    boxes = lax.axis_size("sub")
    part = 4 * slots
    slot_total = sides * boxes * slots
    parity = lax.rem(lax.axis_index("iface"), 2)
    place = (lax.axis_index("sub") + boxes * parity).reshape(1)

    params = pltpu.CompilerParams(vmem_limit_bytes=24 * MIB)
    piece = jax.ShapeDtypeStruct((REACH, rows, fields), BF16)
    toward = jax.ShapeDtypeStruct((boxes, part, fields), BF16)
    to_pair, to_other = pl.pallas_call(
        functools.partial(edge_kernel, boxes),
        out_shape=[piece, piece],
        in_specs=[hbm()] * 3,
        out_specs=[vmem()] * 2,
        scratch_shapes=[
            pltpu.SMEM((1,), INT),
            pltpu.SMEM((1, leaves), INT),
            pltpu.VMEM((2 * REACH, rows, fields), BF16),
            pltpu.SemaphoreType.DMA((4,)),
        ],
        compiler_params=params,
        cost_estimate=COST,
        name="edges",
    )(place, pin(elem_count), pin(traces))
    to_met, to_turn, moment = pl.pallas_call(
        pack_kernel,
        out_shape=(toward, toward, jax.ShapeDtypeStruct((q, fields), BF16)),
        in_specs=[pl.BlockSpec(memory_space=pl.ANY)] + [hbm()] * 5,
        out_specs=(vmem(),) * 3,
        scratch_shapes=[
            pltpu.SMEM((1,), INT),
            pltpu.SMEM((1, leaves), INT),
            pltpu.VMEM(send_idx.shape[2:], INT),
            pltpu.VMEM((leaves, rows, fields), BF16),
            pltpu.VMEM((leaves, q, rows), BF16),
            pltpu.SemaphoreType.DMA((5,)),
        ],
        compiler_params=params,
        cost_estimate=COST,
        name="pack",
    )(to_pair, place, pin(elem_count), pin(send_idx), pin(traces), pin(source_map))

    def flips(bit):
        return [(b, b ^ bit) for b in range(boxes) if b ^ bit < boxes]

    across = [(b, b + 1) for b in range(1, boxes - 1, 2)]
    across = across + [(j, i) for i, j in across]
    first = lax.ppermute(to_pair, "sub", flips(1))
    meet = [(g, g ^ 1) for g in range(groups) if g ^ 1 < groups]
    met = lax.ppermute(to_met, "iface", meet)
    turn = [(g, g + 1) for g in range(1, groups - 1, 2)]
    other = lax.ppermute(to_turn, "iface", turn + [(j, i) for i, j in turn])
    to_other = lax.optimization_barrier((to_other, moment))[0]
    direct = lax.ppermute(to_other, "sub", across)
    carried = lax.optimization_barrier((moment, first))[0]
    carried = jnp.broadcast_to(carried, (boxes, q, fields))
    chunks = jnp.concatenate([met, other, carried], axis=1)
    owned = lax.all_to_all(chunks, "sub", split_axis=0, concat_axis=0, tiled=True)
    near_at = pin(near_idx.transpose(2, 0, 1))
    slot_total = sides * boxes * slots
    acc, slot_rows = pl.pallas_call(
        near_kernel,
        out_shape=(
            jax.ShapeDtypeStruct((leaves, rows, fields), F32),
            jax.ShapeDtypeStruct((8, slot_total), F32),
        ),
        in_specs=[hbm()] * 10,
        out_specs=(vmem(), vmem()),
        scratch_shapes=[
            pltpu.SMEM((1,), INT),
            pltpu.SMEM((1, leaves), INT),
            pltpu.SMEM((near_slots, 1, leaves), INT),
            pltpu.SMEM((1, leaves), INT),
            pltpu.VMEM((sides, boxes, slots), INT),
            pltpu.SMEM((sides, boxes), INT),
            pltpu.VMEM((sides, boxes, slots), F32),
            pltpu.VMEM(near_blocks.shape[1:], BF16),
            pltpu.VMEM((leaves + REACH + 1, rows, fields), BF16),
            pltpu.SemaphoreType.DMA((9,)),
            pltpu.SemaphoreType.DMA((leaves,)),
        ],
        compiler_params=params,
        cost_estimate=COST,
        name="near",
    )(
        lax.optimization_barrier((place, chunks))[0],
        pin(elem_count),
        near_at,
        pin(near_count),
        pin(recv_idx),
        pin(recv_count),
        pin(couple_weight),
        pin(traces),
        pin(near_blocks),
        pin(first),
    )

    out = pl.pallas_call(
        final_kernel,
        out_shape=jax.ShapeDtypeStruct((leaves, rows, fields), BF16),
        in_specs=[hbm()] * 9 + [vmem()] * 4,
        out_specs=hbm(),
        scratch_shapes=[
            pltpu.SMEM((1,), INT),
            pltpu.SMEM((1, leaves), INT),
            pltpu.SMEM((near_slots, 1, leaves), INT),
            pltpu.SMEM((1, leaves), INT),
            pltpu.SMEM((1, 1, translate.shape[2]), INT),
            pltpu.SMEM((1, 1), INT),
            pltpu.VMEM((REACH,) + near_blocks.shape[2:], BF16),
            pltpu.VMEM(translate.shape[2:], BF16),
            pltpu.VMEM((leaves, rows, q), BF16),
            pltpu.VMEM((REACH + 1, rows, fields), BF16),
            pltpu.VMEM((leaves, rows, fields), BF16),
            pltpu.VMEM((leaves, rows, fields), F32),
            pltpu.SemaphoreType.DMA((8,)),
            pltpu.SemaphoreType.DMA((2 + REACH,)),
        ],
        compiler_params=params,
        cost_estimate=COST,
        name="final",
    )(
        place,
        pin(elem_count),
        near_at,
        pin(near_count),
        pin(m2l_idx),
        m2l_count,
        pin(near_blocks),
        pin(translate),
        pin(evaluate),
        acc,
        slot_rows,
        direct,
        owned,
    )
    return out[None]


def solution(mesh):
    def split(rank):
        return P("iface", "sub", *(None,) * (rank - 2))

    return jax.shard_map(
        shards,
        mesh=mesh,
        in_specs=tuple(split(rank) for rank in (4, 2, 3, 2, 5, 4, 3, 2, 5, 4, 5, 5, 4, 5)),
        out_specs=split(4),
        check_vma=False,
    )
```

```python
import functools

import jax
import jax.numpy as jnp
from jax import lax
from jax.experimental import pallas as pl
from jax.experimental.pallas import tpu as pltpu
from jax.sharding import PartitionSpec as P

REACH = 3
MIB = 1 << 20
F32 = jnp.float32
BF16 = jnp.bfloat16
INT = jnp.int32
GROUP = 4
COST = pl.CostEstimate(flops=1, bytes_accessed=1, transcendentals=0)


def dot(a, b):
    return jnp.dot(a, b, preferred_element_type=F32)


def live_rows(count, leaf_size, fields):
    return lax.broadcasted_iota(INT, (leaf_size, fields), 0) < count


def masked_leaf(x, count):
    rows, fields = x.shape
    live = jnp.where(live_rows(count, rows // 4, fields), 1.0, 0.0).astype(BF16)
    return (x.reshape(4, rows // 4, fields) * live[None]).reshape(rows, fields)


def column(values):
    width = values.shape[-1]
    wide = values.astype(F32).reshape(-1, 1, width)
    shape = (wide.shape[0], width, width)
    same = lax.broadcasted_iota(INT, shape, 1) == lax.broadcasted_iota(INT, shape, 2)
    return jnp.sum(jnp.where(same, wide, 0.0), axis=2, keepdims=True).reshape(-1, 1)


def row(col):
    n = col.shape[0]
    same = lax.broadcasted_iota(INT, (n, n), 0) == lax.broadcasted_iota(INT, (n, n), 1)
    return jnp.sum(jnp.where(same, col, 0.0), axis=0, keepdims=True)


def load(pairs, sems):
    copies = [pltpu.make_async_copy(a, b, sems.at[i]) for i, (a, b) in enumerate(pairs)]
    for copy in copies:
        copy.start()
    return copies


def box_of(place, boxes):
    return lax.rem(place, boxes)


def met_side(place, boxes):
    return jnp.where(place < boxes, 1, 0)


def edge_kernel(boxes, place_hbm, count_hbm, x_hbm, pair_ref, other_ref, place_ref, count_ref, x_ref, sems):
    last = x_hbm.shape[1] - REACH
    copies = load(
        [
            (place_hbm, place_ref),
            (count_hbm, count_ref),
            (x_hbm.at[0, 0:REACH], x_ref.at[0:REACH]),
            (x_hbm.at[0, last:], x_ref.at[REACH:]),
        ],
        sems,
    )
    for copy in copies:
        copy.wait()
    odd = lax.rem(box_of(place_ref[0], boxes), 2)
    for i in range(REACH):
        for ref, upper in ((pair_ref, 1 - odd), (other_ref, odd)):
            ref[i] = masked_leaf(x_ref[upper * REACH + i], count_ref[0, upper * last + i])


def pack_kernel(
    after_hbm,
    place_hbm,
    count_hbm,
    send_hbm,
    x_hbm,
    source_hbm,
    met_ref,
    other_ref,
    moment_ref,
    place_ref,
    count_ref,
    send_ref,
    x_ref,
    source_ref,
    sems,
):
    leaves, rows, fields = x_ref.shape
    leaf_size = rows // 4
    sides, boxes, slots = send_ref.shape
    copies = load(
        [
            (place_hbm, place_ref),
            (count_hbm, count_ref),
            (send_hbm.at[0, 0], send_ref),
            (x_hbm.at[0], x_ref),
            (source_hbm.at[0], source_ref),
        ],
        sems,
    )
    for copy in copies[:3]:
        copy.wait()
    met = met_side(place_ref[0], boxes)
    send = jnp.concatenate([send_ref[met], send_ref[1 - met]], axis=0)
    send = column(send).astype(INT)
    total = sides * boxes * slots
    element = lax.broadcasted_iota(INT, (total, leaves * leaf_size), 1)
    at = lax.broadcasted_iota(INT, (1, leaves * leaf_size), 1)
    end = jnp.zeros_like(at)
    for l in range(leaves):
        end = jnp.where(at >= l * leaf_size, l * leaf_size + count_ref[0, l], end)
    pick = jnp.where((element == send) & (at < end), 1.0, 0.0).astype(BF16)
    copies[3].wait()
    for c in range(4):
        comp = x_ref[:, c * leaf_size : (c + 1) * leaf_size, :]
        got = dot(pick, comp.reshape(leaves * leaf_size, fields)).astype(BF16)
        for s, ref in enumerate((met_ref, other_ref)):
            for o in range(boxes):
                at = (s * boxes + o) * slots
                ref[o, c * slots : (c + 1) * slots, :] = got[at : at + slots]
    for l in range(leaves):
        x_ref[l] = masked_leaf(x_ref[l], count_ref[0, l])
    copies[4].wait()
    blocks = jnp.concatenate([source_ref[l] for l in range(leaves)], axis=1)
    moment = dot(blocks, x_ref[...].reshape(leaves * rows, fields)).astype(BF16)
    moment_ref[...] = moment


def near_kernel(
    place_hbm,
    count_hbm,
    idx_hbm,
    live_hbm,
    recv_hbm,
    recv_count_hbm,
    weight_hbm,
    x_hbm,
    near_hbm,
    first_hbm,
    acc_ref,
    rows_ref,
    place_ref,
    count_ref,
    idx_ref,
    live_ref,
    recv_ref,
    recv_count_ref,
    weight_ref,
    near_ref,
    src_ref,
    sems,
    near_sems,
):
    leaves, rows, fields = acc_ref.shape
    leaf_size = rows // 4
    near_slots = idx_ref.shape[0]
    sides, boxes, slots = recv_ref.shape
    copies = load(
        [
            (place_hbm, place_ref),
            (count_hbm, count_ref),
            (recv_hbm.at[0, 0], recv_ref),
            (recv_count_hbm.at[0, 0], recv_count_ref),
            (weight_hbm.at[0, 0], weight_ref),
            (idx_hbm, idx_ref),
            (live_hbm, live_ref),
            (x_hbm.at[0], src_ref.at[0:leaves]),
            (first_hbm, src_ref.at[leaves : leaves + REACH]),
        ],
        sems,
    )
    near_copies = load([(near_hbm.at[0, l], near_ref.at[l]) for l in range(leaves)], near_sems)
    zero_leaf = leaves + REACH
    src_ref[zero_leaf] = jnp.zeros((rows, fields), BF16)
    for copy in copies[:7]:
        copy.wait()

    met = met_side(place_ref[0], boxes)
    weights = []
    for s in (met, 1 - met):
        for b in range(boxes):
            live = lax.broadcasted_iota(INT, (1, slots), 1) < recv_count_ref[s, b]
            weights.append(jnp.where(live, weight_ref[s, b : b + 1, :], 0.0))
    weight = row(column(jnp.concatenate(weights, axis=0)))
    target = jnp.concatenate([recv_ref[met], recv_ref[1 - met]], axis=0)
    target = row(column(target))
    upper = weight.astype(BF16).astype(F32)
    rows_ref[0:1, :] = target
    rows_ref[1:2, :] = upper
    rows_ref[2:3, :] = weight - upper

    copies[7].wait()
    copies[8].wait()
    for l in range(leaves):
        src_ref[l] = masked_leaf(src_ref[l], count_ref[0, l])
    me = box_of(place_ref[0], boxes)
    odd = lax.rem(me, 2) == 1
    start = me * leaves
    for l in range(leaves):
        if l % GROUP == 0:
            for copy in near_copies[l : l + GROUP]:
                copy.wait()
        blocks, sources = [], []
        for s in range(near_slots):
            at = idx_ref[s, 0, l] - start
            pair = jnp.where(odd, at < 0, at >= leaves)
            own = (at >= 0) & (at < leaves)
            at = at + jnp.where(pair & odd, leaves + REACH, 0)
            used = (s < live_ref[0, l]) & (own | pair)
            blocks.append(near_ref[l, s])
            sources.append(src_ref[jnp.where(used, at, zero_leaf)])
        acc_ref[l] = dot(jnp.concatenate(blocks, axis=1), jnp.concatenate(sources, axis=0))


def final_kernel(
    place_hbm,
    count_hbm,
    idx_hbm,
    live_hbm,
    m2l_hbm,
    m2l_count_hbm,
    near_hbm,
    translate_hbm,
    evaluate_hbm,
    acc_ref,
    rows_ref,
    direct_ref,
    owned_ref,
    out_hbm,
    place_ref,
    count_ref,
    idx_ref,
    live_ref,
    m2l_ref,
    m2l_count_ref,
    near_ref,
    translate_ref,
    evaluate_ref,
    halo_ref,
    out_ref,
    part_ref,
    sems,
    out_sems,
):
    leaves, rows, fields = out_ref.shape
    leaf_size = rows // 4
    near_slots = idx_ref.shape[0]
    boxes, chunk, _ = owned_ref.shape
    q = translate_ref.shape[1]
    part = (chunk - q) // 2
    slots = part // 4
    copies = load(
        [
            (place_hbm, place_ref),
            (m2l_hbm, m2l_ref),
            (m2l_count_hbm, m2l_count_ref),
            (count_hbm, count_ref),
            (idx_hbm, idx_ref),
            (live_hbm, live_ref),
            (translate_hbm.at[0, 0], translate_ref),
            (evaluate_hbm.at[0], evaluate_ref),
        ],
        sems,
    )
    zero_leaf = REACH
    halo_ref[zero_leaf] = jnp.zeros((rows, fields), BF16)
    copies[0].wait()
    place = place_ref[0]
    me = box_of(place, boxes)
    odd = lax.rem(me, 2)
    edge = odd * (leaves - REACH)
    near_copy = pltpu.make_async_copy(near_hbm.at[0, pl.ds(edge, REACH)], near_ref, out_sems.at[0])
    near_copy.start()

    for i in range(REACH):
        halo_ref[i] = direct_ref[i]

    slot_total = rows_ref.shape[1]
    element = lax.broadcasted_iota(INT, (leaves * leaf_size, slot_total), 0)
    hit = element == rows_ref[0:1, :].astype(INT)
    spread = jnp.concatenate(
        [jnp.where(hit, rows_ref[i : i + 1, :], 0.0).astype(BF16) for i in (1, 2)], axis=1
    )
    for c in range(4):
        comp = [
            owned_ref[:, at : at + slots, :].reshape(boxes * slots, fields)
            for at in (c * slots, part + c * slots)
        ]
        sums = dot(spread, jnp.concatenate(comp + comp, axis=0))
        sums = sums if c < 2 else -sums
        part_ref[:, c * leaf_size : (c + 1) * leaf_size, :] = sums.reshape(
            leaves, leaf_size, fields
        )

    for copy in copies[1:]:
        copy.wait()
    local = jnp.zeros((q, fields), F32)
    for t in range(translate_ref.shape[0]):
        moment = owned_ref[m2l_ref[0, 0, t], 2 * part :, :]
        moment = jnp.where(t < m2l_count_ref[0, 0], moment.astype(F32), 0.0).astype(BF16)
        local += dot(translate_ref[t], moment)
    local = local.astype(BF16)
    def finish(l, total):
        total = (total + acc_ref[l] + part_ref[l]).reshape(4, leaf_size, fields)
        live = live_rows(count_ref[0, l], leaf_size, fields)
        out_ref[l] = jnp.where(live[None], total, 0.0).astype(BF16).reshape(rows, fields)

    start = me * leaves
    inner = leaves - REACH

    def sums(parity):
        first_far = parity * inner
        rest = (1 - parity) * REACH
        stores = []

        def store(at, size):
            span = slice(at, at + size)
            copy = pltpu.make_async_copy(
                out_ref.at[span], out_hbm.at[span], out_sems.at[1 + len(stores)]
            )
            copy.start()
            stores.append(copy)

        for l in range(rest, rest + inner):
            finish(l, dot(evaluate_ref[l], local))
        store(rest, inner)
        near_copy.wait()
        for i in range(REACH):
            l = first_far + i
            blocks, sources = [], []
            for s in range(near_slots):
                at = idx_ref[s, 0, l] - start
                far = at >= leaves if parity else at < 0
                at = at + (-leaves if parity else REACH)
                used = (s < live_ref[0, l]) & far
                blocks.append(near_ref[i, s])
                sources.append(halo_ref[jnp.where(used, at, zero_leaf)])
            blocks.append(evaluate_ref[l])
            sources.append(local)
            finish(l, dot(jnp.concatenate(blocks, axis=1), jnp.concatenate(sources, axis=0)))
            store(l, 1)
        for copy in stores:
            copy.wait()

    for parity in (0, 1):
        pl.when(odd == parity)(functools.partial(sums, parity))


def vmem():
    return pl.BlockSpec(memory_space=pltpu.VMEM)


def hbm():
    return pl.BlockSpec(memory_space=pltpu.MemorySpace.HBM)


def pin(x):
    return pltpu.with_memory_space_constraint(x, pltpu.MemorySpace.HBM)


def shards(
    traces,
    elem_count,
    near_idx,
    near_count,
    near_blocks,
    source_map,
    m2l_idx,
    m2l_count,
    translate,
    evaluate,
    send_idx,
    recv_idx,
    recv_count,
    couple_weight,
):
    leaves, rows, fields = traces.shape[1:]
    q = source_map.shape[2]
    sides, _, slots = send_idx.shape[2:]
    near_slots = near_idx.shape[2]
    groups = lax.axis_size("iface")
    boxes = lax.axis_size("sub")
    part = 4 * slots
    slot_total = sides * boxes * slots
    parity = lax.rem(lax.axis_index("iface"), 2)
    place = (lax.axis_index("sub") + boxes * parity).reshape(1)

    params = pltpu.CompilerParams(vmem_limit_bytes=24 * MIB)
    piece = jax.ShapeDtypeStruct((REACH, rows, fields), BF16)
    toward = jax.ShapeDtypeStruct((boxes, part, fields), BF16)
    to_pair, to_other = pl.pallas_call(
        functools.partial(edge_kernel, boxes),
        out_shape=[piece, piece],
        in_specs=[hbm()] * 3,
        out_specs=[vmem()] * 2,
        scratch_shapes=[
            pltpu.SMEM((1,), INT),
            pltpu.SMEM((1, leaves), INT),
            pltpu.VMEM((2 * REACH, rows, fields), BF16),
            pltpu.SemaphoreType.DMA((4,)),
        ],
        compiler_params=params,
        cost_estimate=COST,
        name="edges",
    )(place, pin(elem_count), pin(traces))
    to_met, to_turn, moment = pl.pallas_call(
        pack_kernel,
        out_shape=(toward, toward, jax.ShapeDtypeStruct((q, fields), BF16)),
        in_specs=[pl.BlockSpec(memory_space=pl.ANY)] + [hbm()] * 5,
        out_specs=(vmem(),) * 3,
        scratch_shapes=[
            pltpu.SMEM((1,), INT),
            pltpu.SMEM((1, leaves), INT),
            pltpu.VMEM(send_idx.shape[2:], INT),
            pltpu.VMEM((leaves, rows, fields), BF16),
            pltpu.VMEM((leaves, q, rows), BF16),
            pltpu.SemaphoreType.DMA((5,)),
        ],
        compiler_params=params,
        cost_estimate=COST,
        name="pack",
    )(to_pair, place, pin(elem_count), pin(send_idx), pin(traces), pin(source_map))

    def flips(bit):
        return [(b, b ^ bit) for b in range(boxes) if b ^ bit < boxes]

    across = [(b, b + 1) for b in range(1, boxes - 1, 2)]
    across = across + [(j, i) for i, j in across]
    first = lax.ppermute(to_pair, "sub", flips(1))
    meet = [(g, g ^ 1) for g in range(groups) if g ^ 1 < groups]
    met = lax.ppermute(to_met, "iface", meet)
    turn = [(g, g + 1) for g in range(1, groups - 1, 2)]
    other = lax.ppermute(to_turn, "iface", turn + [(j, i) for i, j in turn])
    to_other = lax.optimization_barrier((to_other, moment))[0]
    direct = lax.ppermute(to_other, "sub", across)
    carried = lax.optimization_barrier((moment, first))[0]
    carried = jnp.broadcast_to(carried, (boxes, q, fields))
    chunks = jnp.concatenate([met, other, carried], axis=1)
    owned = lax.all_to_all(chunks, "sub", split_axis=0, concat_axis=0, tiled=True)
    near_at = pin(near_idx.transpose(2, 0, 1))
    slot_total = sides * boxes * slots
    acc, slot_rows = pl.pallas_call(
        near_kernel,
        out_shape=(
            jax.ShapeDtypeStruct((leaves, rows, fields), F32),
            jax.ShapeDtypeStruct((8, slot_total), F32),
        ),
        in_specs=[hbm()] * 10,
        out_specs=(vmem(), vmem()),
        scratch_shapes=[
            pltpu.SMEM((1,), INT),
            pltpu.SMEM((1, leaves), INT),
            pltpu.SMEM((near_slots, 1, leaves), INT),
            pltpu.SMEM((1, leaves), INT),
            pltpu.VMEM((sides, boxes, slots), INT),
            pltpu.SMEM((sides, boxes), INT),
            pltpu.VMEM((sides, boxes, slots), F32),
            pltpu.VMEM(near_blocks.shape[1:], BF16),
            pltpu.VMEM((leaves + REACH + 1, rows, fields), BF16),
            pltpu.SemaphoreType.DMA((9,)),
            pltpu.SemaphoreType.DMA((leaves,)),
        ],
        compiler_params=params,
        cost_estimate=COST,
        name="near",
    )(
        lax.optimization_barrier((place, chunks))[0],
        pin(elem_count),
        near_at,
        pin(near_count),
        pin(recv_idx),
        pin(recv_count),
        pin(couple_weight),
        pin(traces),
        pin(near_blocks),
        pin(first),
    )

    out = pl.pallas_call(
        final_kernel,
        out_shape=jax.ShapeDtypeStruct((leaves, rows, fields), BF16),
        in_specs=[hbm()] * 9 + [vmem()] * 4,
        out_specs=hbm(),
        scratch_shapes=[
            pltpu.SMEM((1,), INT),
            pltpu.SMEM((1, leaves), INT),
            pltpu.SMEM((near_slots, 1, leaves), INT),
            pltpu.SMEM((1, leaves), INT),
            pltpu.SMEM((1, 1, translate.shape[2]), INT),
            pltpu.SMEM((1, 1), INT),
            pltpu.VMEM((REACH,) + near_blocks.shape[2:], BF16),
            pltpu.VMEM(translate.shape[2:], BF16),
            pltpu.VMEM((leaves, rows, q), BF16),
            pltpu.VMEM((REACH + 1, rows, fields), BF16),
            pltpu.VMEM((leaves, rows, fields), BF16),
            pltpu.VMEM((leaves, rows, fields), F32),
            pltpu.SemaphoreType.DMA((8,)),
            pltpu.SemaphoreType.DMA((2 + REACH,)),
        ],
        compiler_params=params,
        cost_estimate=COST,
        name="final",
    )(
        place,
        pin(elem_count),
        near_at,
        pin(near_count),
        pin(m2l_idx),
        m2l_count,
        pin(near_blocks),
        pin(translate),
        pin(evaluate),
        acc,
        slot_rows,
        direct,
        owned,
    )
    return out[None]


def solution(mesh):
    def split(rank):
        return P("iface", "sub", *(None,) * (rank - 2))

    return jax.shard_map(
        shards,
        mesh=mesh,
        in_specs=tuple(split(rank) for rank in (4, 2, 3, 2, 5, 4, 3, 2, 5, 4, 5, 5, 4, 5)),
        out_specs=split(4),
        check_vma=False,
    )
```
